1024 devices in a mesh: dp: 64 (over y, z_lo, core), tensor: 16 (over x, z_hi).
Axes of the slice: x: 4, y: 4, z: 32 (z_hi: 4, z_lo: 8; z = z_hi * 8 + z_lo), core: 2. Of those that a mesh axis runs over, the one named last changes fastest.
Arguments:
- inputs: bfloat16 [128, 9216], P('tensor', 'dp'), may hold values from -6 to 6
- grad_out: bfloat16 [128, 9216], P('tensor', 'dp'), may hold values from -3 to 3
- saved_pre: bfloat16 [128, 36864], P('dp', 'tensor'), may hold values from -8 to 8
- w_in: bfloat16 [9216, 36864], P('dp', 'tensor'), may hold values from -0.0625 to 0.0625
- w_out: bfloat16 [36864, 9216], P('tensor', 'dp'), may hold values from -0.03125 to 0.03125
Outputs:
- grad_in: bfloat16 [128, 9216], P('tensor', 'dp')
- grad_w_in: bfloat16 [9216, 36864], P('dp', 'tensor')
- grad_w_out: bfloat16 [36864, 9216], P('tensor', 'dp')
The draws below stay inside these ranges and needn't reach their ends.
All inputs are finite; a program needn't handle non-finite values.
Results may differ from the reference program's by a relative error of at most 0.015.
Values may be sent and summed in bfloat16 or wider, within the bound.
A program may use at most 32 MiB of HBM per device.

```python
import jax
import jax.numpy as jnp
from jax import lax

D = 9216
F = 36864
TOKENS = 128


def block_scale(own_key, dims, cuts, smallest, top_value):
    level = 1.0
    for dim, blocks in cuts:
        draws = jax.random.uniform(jax.random.fold_in(jax.random.fold_in(own_key, 6), dim), (blocks,), jnp.float32, smallest / len(cuts), top_value / len(cuts))
        level = level * jnp.repeat(jnp.exp(draws), dims[dim] // blocks).reshape((-1,) + (1,) * (len(dims) - 1 - dim))
    return level


def bell_draw(key, dims, scale, limit, pieces=(), held_as=jnp.bfloat16):
    gain = block_scale(key, dims, pieces, -0.22, 0.18) if pieces else 1.0
    array = jax.random.normal(key, dims, jnp.float32) * scale * gain
    return jnp.minimum(jnp.maximum(array, -limit), limit).astype(held_as)


def setup_inputs(seed: int = 0) -> dict:
    key_list = jax.random.split(jax.random.key(seed), 6)
    inputs = bell_draw(key_list[0], (TOKENS, D), 1.0, 6.0, ((0, 16), (1, 64)))
    grad_out = bell_draw(key_list[1], (TOKENS, D), 0.5, 3.0, ((0, 16), (1, 64)))
    saved_pre = bell_draw(key_list[2], (TOKENS, F), 1.5, 8.0, ((0, 64), (1, 16)))
    w_in = bell_draw(key_list[3], (D, F), D ** -0.5, 0.0625, ((0, 64), (1, 16)))
    w_out = bell_draw(key_list[4], (F, D), F ** -0.5, 0.03125, ((0, 16), (1, 64)))
    return dict(inputs=inputs, grad_out=grad_out, saved_pre=saved_pre, w_in=w_in, w_out=w_out)


root_half = 0.7071067811865476
inv_root_two_pi = 0.3989422804014327


def gelu_parts(saved):
    value = saved.astype(jnp.float32)
    cdf = 0.5 * (1.0 + lax.erf(value * root_half))
    density = inv_root_two_pi * jnp.exp(-0.5 * value * value)
    return value * cdf, cdf + value * density


def reference(inputs, grad_out, saved_pre, w_in, w_out):
    activated, slope = gelu_parts(saved_pre)
    hidden_act = activated.astype(jnp.bfloat16)
    grad_hidden = jnp.dot(grad_out, w_out.T, preferred_element_type=jnp.float32)
    grad_pre = (grad_hidden * slope).astype(jnp.bfloat16)
    grad_in = jnp.dot(grad_pre, w_in.T, preferred_element_type=jnp.float32).astype(jnp.bfloat16)
    grad_w_in = jnp.dot(inputs.T, grad_pre, preferred_element_type=jnp.float32).astype(jnp.bfloat16)
    grad_w_out = jnp.dot(hidden_act.T, grad_out, preferred_element_type=jnp.float32).astype(jnp.bfloat16)
    return grad_in, grad_w_in, grad_w_out
```

```python
import functools

import jax
import jax.numpy as jnp
from jax import lax
from jax.experimental import pallas as pl
from jax.experimental.pallas import tpu as pltpu
from jax.sharding import PartitionSpec as P

GRID = dict(ny=4, nz=8, nx=4, nh=4)

root_half = 0.7071067811865476
inv_root_two_pi = 0.3989422804014327
bf16, f32 = jnp.bfloat16, jnp.float32


def gelu_parts(saved):
    value = saved.astype(f32)
    cdf = 0.5 * (1.0 + lax.erf(value * root_half))
    density = inv_root_two_pi * jnp.exp(-0.5 * value * value)
    return value * cdf, cdf + value * density


def kernel(
    ny, nz, nx, nh,
    x_hbm, g_hbm, s_hbm, wi_hbm, wo_hbm,
    gin_hbm, gwi_hbm, gwo_hbm,
    rows, own_s, peer_s, wi_v, wo_v, wide, grad_rows, input_rows,
    slope, quad, hid, pre,
    b1_send, b1_recv, b1_own, b2_send, b2_recv, b2_sum, b3_send, b3_own, b3_recv,
    pack, hid_full, pre_full, gwi_v, gwo_v,
    dx_part, dx_send, dx_recv, dz_part, dz_send, dz_recv, gin_v,
    local_sem, send_sem,
    az_sem, ax_sem, s_sem, hz_sem, hy_sem, hc_sem,
    b1_sem, b2_sem, b3_sem, c1_sem, c2_sem, c3_sem, dx_sem, dz_sem,
):
    dp, tp = lax.axis_index("dp"), lax.axis_index("tensor")
    core = lax.rem(dp, 2)
    chip = lax.div(dp, 2)
    z, y = lax.rem(chip, nz), lax.div(chip, nz)
    x, h = lax.div(tp, nh), lax.rem(tp, nh)
    other = 1 - core

    def at(y=y, z=z, core=core, x=x, h=h):
        return {"dp": (y * nz + z) * 2 + core, "tensor": x * nh + h}

    y_peer = [None] + [at(y=lax.rem(y + k, ny)) for k in range(1, ny)]
    z_peer = [None] + [at(z=lax.rem(z + k, nz)) for k in range(1, nz)]
    x_peer = [None] + [at(x=lax.rem(x + k, nx)) for k in range(1, nx)]
    right, left = at(h=lax.rem(h + 1, nh)), at(h=lax.rem(h + nh - 1, nh))
    partner = at(core=other)
    peers = y_peer[1:] + z_peer[1:] + x_peer[1:] + [right, left, partner]

    half = wi_v.shape[2]
    width = wi_v.shape[1]
    tokens = b1_send.shape[0] * b1_send.shape[1]

    loads = []

    def load(src, dst):
        copy = pltpu.make_async_copy(src, dst, local_sem.at[len(loads)])
        copy.start()
        loads.append(copy)
        return copy

    load_g = load(g_hbm, rows.at[tp, 0])
    load_x = load(x_hbm, rows.at[tp, 1])
    load_s = [load(s_hbm.at[:, pl.ds(i * half, half)], own_s.at[i]) for i in range(2)]
    load_wo = [load(wo_hbm.at[:, pl.ds(i * half, half)], wo_v.at[i]) for i in range(2)]
    load_wi = [load(wi_hbm.at[:, pl.ds(i * half, half)], wi_v.at[i]) for i in range(2)]

    barrier = pltpu.get_barrier_semaphore()
    for peer in peers:
        pl.semaphore_signal(barrier, inc=1, device_id=peer, device_id_type=pl.DeviceIdType.MESH)
    pl.semaphore_wait(barrier, len(peers))

    sends = []

    def send(src, dst, recv_sem, peer):
        copy = pltpu.make_async_remote_copy(
            src_ref=src, dst_ref=dst, send_sem=send_sem.at[len(sends)], recv_sem=recv_sem,
            device_id=peer, device_id_type=pl.DeviceIdType.MESH,
        )
        copy.start()
        sends.append(copy)

    def arrived(dst, recv_sem):
        pltpu.make_async_remote_copy(
            src_ref=dst, dst_ref=dst, send_sem=send_sem.at[0], recv_sem=recv_sem,
            device_id=partner, device_id_type=pl.DeviceIdType.MESH,
        ).wait_recv()

    slot = lambda x_, h_: x_ * nh + h_
    h_left, h_right, h_far = lax.rem(h + nh - 1, nh), lax.rem(h + 1, nh), lax.rem(h + 2, nh)

    def to_x(which, h_):
        block = rows.at[slot(x, h_)]
        for k in range(1, nx):
            send(block, block, ax_sem.at[k - 1, which], x_peer[k])

    load_g.wait()
    load_x.wait()
    mine = rows.at[tp]
    send(mine, mine, az_sem.at[0], right)
    send(mine, mine, az_sem.at[1], left)

    for copy in load_s:
        copy.wait()
    send(own_s.at[other], peer_s, s_sem.at[0], partner)
    to_x(0, h)

    arrived(peer_s, s_sem.at[0])
    own, peer = gelu_parts(own_s[core]), gelu_parts(peer_s[...])
    n = own[0].shape[0]
    first = core == 0
    for ref, i in ((quad, 0), (slope, 1)):
        ref[0:n, :] = jnp.where(first, own[i], peer[i])
        ref[n : 2 * n, :] = jnp.where(first, peer[i], own[i])
    hid[core, y, z] = quad[...].astype(bf16)

    def to_z(buf, sem):
        block = buf.at[core, y, z]
        for k in range(1, nz):
            send(block, block, sem.at[k - 1], z_peer[k])

    def from_z(buf, sem):
        for k in range(1, nz):
            arrived(buf.at[core, y, lax.rem(z + nz - k, nz)], sem.at[k - 1])

    def to_y(buf, sem):
        block = buf.at[core, y]
        for k in range(1, ny):
            send(block, block, sem.at[k - 1], y_peer[k])

    def from_y(buf, sem, k):
        arrived(buf.at[core, lax.rem(y + ny - k, ny)], sem.at[k - 1])

    to_z(hid, hz_sem)

    from_left = rows.at[slot(x, h_left)]
    arrived(from_left, az_sem.at[0])
    send(from_left, from_left, az_sem.at[2], right)
    to_x(1, h_left)
    arrived(rows.at[slot(x, h_right)], az_sem.at[1])
    to_x(2, h_right)
    from_z(hid, hz_sem)
    to_y(hid, hy_sem)
    arrived(rows.at[slot(x, h_far)], az_sem.at[2])
    to_x(3, h_far)
    for copy in load_wo:
        copy.wait()
    for which, h_ in enumerate((h, h_left, h_right, h_far)):
        for k in range(1, nx):
            arrived(rows.at[slot(lax.rem(x + nx - k, nx), h_)], ax_sem.at[k - 1, which])

    def gathered(which, out):
        step = rows.shape[2]
        for t in range(rows.shape[0]):
            wide[t * step : (t + 1) * step, :] = rows[t, which].astype(f32)
        out[...] = wide[...].astype(bf16)

    gathered(0, grad_rows)

    def product(which):
        return jnp.dot(grad_rows[...], wo_v[which], preferred_element_type=f32)

    b1_send[...] = product(other).astype(bf16).reshape(b1_send.shape)
    for k in list(range(1, ny)) + [0]:
        y_ = lax.rem(y + k, ny)
        send(b1_send.at[y_], b1_recv.at[y_], b1_sem.at[k], partner)
    b1_own[...] = product(core).reshape(b1_own.shape)
    for k in range(1, ny):
        from_y(hid, hy_sem, k)
    for k in list(range(1, ny)) + [0]:
        y_ = lax.rem(y + k, ny)
        arrived(b1_recv.at[y_], b1_sem.at[k])
        total = b1_own[y_] + b1_recv[y_].astype(f32)
        if k:
            b2_send[k - 1] = total.astype(bf16)
            send(b2_send.at[k - 1], b2_recv.at[k - 1], b2_sem.at[k - 1], y_peer[k])
        else:
            b2_sum[...] = total
    send(hid.at[core], hid.at[core], hc_sem.at[0], partner)
    for k in range(1, ny):
        arrived(b2_recv.at[k - 1], b2_sem.at[k - 1])
    total = b2_sum[...]
    for k in range(1, ny):
        total = total + b2_recv[k - 1].astype(f32)
    b2_sum[...] = total
    deep = b3_own.shape[1]
    for j in range(nz):
        piece = b2_sum[j * deep : (j + 1) * deep, :]
        b3_own[j] = piece
        b3_send[j] = piece.astype(bf16)
    for k in range(1, nz):
        send(b3_send.at[lax.rem(z + k, nz)], b3_recv.at[k - 1], b3_sem.at[k - 1], z_peer[k])
    total = b3_own[z]
    for k in range(1, nz):
        arrived(b3_recv.at[k - 1], b3_sem.at[k - 1])
        total = total + b3_recv[k - 1].astype(f32)
    pre[core, y, z] = (total * slope[...]).astype(bf16)

    to_z(pre, c1_sem)
    gathered(1, input_rows)
    from_z(pre, c1_sem)
    to_y(pre, c2_sem)
    send(pre.at[core, y], pre.at[core, y], c3_sem.at[0], partner)
    for k in range(1, ny):
        from_y(pre, c2_sem, k)
        block = pre.at[core, lax.rem(y + ny - k, ny)]
        send(block, block, c3_sem.at[k], partner)

    def packed(buf, which, out):
        for i in range(ny):
            for j in range(nz):
                r = (i * nz + j) * deep
                pack[r : r + deep, :] = buf[which, i, j].astype(f32)
        out[which] = pack[...].astype(bf16)

    def back(which):
        return lax.dot_general(
            pre_full[which], wi_v[which], (((1,), (1,)), ((), ())), preferred_element_type=f32
        )

    for copy in load_wi:
        copy.wait()
    packed(pre, core, pre_full)
    part = back(core)
    for k in range(ny):
        arrived(pre.at[other, lax.rem(y + ny - k, ny)], c3_sem.at[k])
    packed(pre, other, pre_full)
    part = part + back(other)

    dx_part[...] = part.reshape(dx_part.shape)
    for k in range(1, nx):
        dx_send[k - 1] = dx_part[lax.rem(x + k, nx)].astype(bf16)
        send(dx_send.at[k - 1], dx_recv.at[k - 1], dx_sem.at[k - 1], x_peer[k])
    arrived(hid.at[other], hc_sem.at[0])
    packed(hid, 0, hid_full)
    packed(hid, 1, hid_full)
    total = dx_part[x]
    for k in range(1, nx):
        arrived(dx_recv.at[k - 1], dx_sem.at[k - 1])
        total = total + dx_recv[k - 1].astype(f32)
    dz_part[...] = total.reshape(dz_part.shape)
    dz_send[0] = dz_part[h_far].astype(bf16)
    dz_send[1] = dz_part[h_left].astype(bf16)
    send(dz_send.at[0], dz_recv.at[0], dz_sem.at[0], right)
    send(dz_send.at[1], dz_recv.at[1], dz_sem.at[1], left)

    def outer(a, b):
        return lax.dot_general(
            a[...], b, (((0,), (0,)), ((), ())), preferred_element_type=f32
        ).astype(bf16)

    for i in range(2):
        gwi_v[:, i * half : (i + 1) * half] = outer(input_rows, pre_full[i])
    out_wi = load(gwi_v, gwi_hbm)
    arrived(dz_recv.at[0], dz_sem.at[0])
    dz_send[2] = (dz_part[h_right] + dz_recv[0].astype(f32)).astype(bf16)
    send(dz_send.at[2], dz_recv.at[2], dz_sem.at[2], right)
    for i in range(2):
        gwo_v[:, i * half : (i + 1) * half] = outer(grad_rows, hid_full[i])
    out_wo = load(gwo_v, gwo_hbm)
    arrived(dz_recv.at[1], dz_sem.at[1])
    arrived(dz_recv.at[2], dz_sem.at[2])
    gin_v[...] = (dz_part[h] + dz_recv[1].astype(f32) + dz_recv[2].astype(f32)).astype(bf16)
    out_in = load(gin_v, gin_hbm)
    for copy in sends:
        copy.wait_send()
    for copy in (out_wi, out_wo, out_in):
        copy.wait()


def on_device(inputs, grad_out, saved_pre, w_in, w_out):
    ny, nz, nx, nh = (GRID[k] for k in ("ny", "nz", "nx", "nh"))
    step, width = inputs.shape
    n, hidden = saved_pre.shape
    half = hidden // 2
    tokens = step * nx * nh
    deep = tokens // (ny * nz)
    per_y, per_x = tokens // ny, tokens // nx
    vmem, dma = pltpu.VMEM, pltpu.SemaphoreType.DMA
    any_space = pl.BlockSpec(memory_space=pl.ANY)
    n_sends = 3 + 4 * (nx - 1) + 1 + 3 * (nz - 1) + 3 * (ny - 1) + ny + 1 + ny + (nx - 1) + 3
    grad_in, grad_w_in, grad_w_out = pl.pallas_call(
        functools.partial(kernel, ny, nz, nx, nh),
        out_shape=(
            jax.ShapeDtypeStruct((step, width), bf16),
            jax.ShapeDtypeStruct((width, hidden), bf16),
            jax.ShapeDtypeStruct((width, hidden), bf16),
        ),
        in_specs=[any_space] * 5,
        out_specs=(any_space,) * 3,
        scratch_shapes=[
            vmem((nx * nh, 2, step, width), bf16),
            vmem((2, n, half), bf16),
            vmem((n, half), bf16),
            vmem((2, width, half), bf16),
            vmem((2, width, half), bf16),
            vmem((tokens, width), f32),
            vmem((tokens, width), bf16),
            vmem((tokens, width), bf16),
            vmem((deep, half), f32),
            vmem((deep, half), f32),
            vmem((2, ny, nz, deep, half), bf16),
            vmem((2, ny, nz, deep, half), bf16),
            vmem((ny, per_y, half), bf16),
            vmem((ny, per_y, half), bf16),
            vmem((ny, per_y, half), f32),
            vmem((ny - 1, per_y, half), bf16),
            vmem((ny - 1, per_y, half), bf16),
            vmem((per_y, half), f32),
            vmem((nz, deep, half), bf16),
            vmem((nz, deep, half), f32),
            vmem((nz - 1, deep, half), bf16),
            vmem((tokens, half), f32),
            vmem((2, tokens, half), bf16),
            vmem((2, tokens, half), bf16),
            vmem((width, hidden), bf16),
            vmem((width, hidden), bf16),
            vmem((nx, per_x, width), f32),
            vmem((nx - 1, per_x, width), bf16),
            vmem((nx - 1, per_x, width), bf16),
            vmem((nh, step, width), f32),
            vmem((3, step, width), bf16),
            vmem((3, step, width), bf16),
            vmem((step, width), bf16),
            dma((11,)),
            dma((n_sends,)),
            dma((3,)),
            dma((nx - 1, 4)),
            dma((1,)),
            dma((nz - 1,)),
            dma((ny - 1,)),
            dma((1,)),
            dma((ny,)),
            dma((ny - 1,)),
            dma((nz - 1,)),
            dma((nz - 1,)),
            dma((ny - 1,)),
            dma((ny,)),
            dma((nx - 1,)),
            dma((3,)),
        ],
        compiler_params=pltpu.CompilerParams(
            collective_id=0, has_side_effects=True, vmem_limit_bytes=48 * 1024 * 1024
        ),
    )(inputs, grad_out, saved_pre, w_in, w_out.T)
    return grad_in, grad_w_in, grad_w_out.T


def solution(mesh):
    return jax.shard_map(
        on_device,
        mesh=mesh,
        in_specs=(
            P("tensor", "dp"),
            P("tensor", "dp"),
            P("dp", "tensor"),
            P("dp", "tensor"),
            P("tensor", "dp"),
        ),
        out_specs=(P("tensor", "dp"), P("dp", "tensor"), P("tensor", "dp")),
        check_vma=False,
    )
```

```python
import functools

import jax
import jax.numpy as jnp
from jax import lax
from jax.experimental import pallas as pl
from jax.experimental.pallas import tpu as pltpu
from jax.sharding import PartitionSpec as P

GRID = dict(ny=4, nz=8, nx=4, nh=4)

root_half = 0.7071067811865476
inv_root_two_pi = 0.3989422804014327
bf16, f32 = jnp.bfloat16, jnp.float32


def gelu_parts(saved):
    value = saved.astype(f32)
    cdf = 0.5 * (1.0 + lax.erf(value * root_half))
    density = inv_root_two_pi * jnp.exp(-0.5 * value * value)
    return value * cdf, cdf + value * density


def kernel(
    ny, nz, nx, nh,
    x_hbm, g_hbm, s_hbm, wi_hbm, wo_hbm,
    gin_v, gwi_v, gwo_v,
    rows, own_s, peer_s, wi_v, wo_v, wide, grad_rows, input_rows,
    slope, quad, hid, pre,
    b1_send, b1_recv, b1_own, b2_send, b2_recv, b2_sum, b2_rows, b3_send, b3_own, b3_recv,
    pack, hid_full, pre_full,
    dx_part, dx_send, dx_recv, dz_part, dz_send, dz_recv,
    local_sem, send_sem,
    az_sem, ax_sem, s_sem, hz_sem, hy_sem, hc_sem,
    b1_sem, b2_sem, b3_sem, c1_sem, c2_sem, c3_sem, dx_sem, dz_sem,
):
    dp, tp = lax.axis_index("dp"), lax.axis_index("tensor")
    core = lax.rem(dp, 2)
    chip = lax.div(dp, 2)
    z, y = lax.rem(chip, nz), lax.div(chip, nz)
    x, h = lax.div(tp, nh), lax.rem(tp, nh)
    other = 1 - core

    def at(y=y, z=z, core=core, x=x, h=h):
        return {"dp": (y * nz + z) * 2 + core, "tensor": x * nh + h}

    y_peer = [None] + [at(y=lax.rem(y + k, ny)) for k in range(1, ny)]
    z_peer = [None] + [at(z=lax.rem(z + k, nz)) for k in range(1, nz)]
    x_peer = [None] + [at(x=lax.rem(x + k, nx)) for k in range(1, nx)]
    right, left = at(h=lax.rem(h + 1, nh)), at(h=lax.rem(h + nh - 1, nh))
    partner = at(core=other)
    peers = y_peer[1:] + z_peer[1:] + x_peer[1:] + [right, left, partner]

    half = wi_v.shape[2]

    loads = []

    def load(src, dst):
        copy = pltpu.make_async_copy(src, dst, local_sem.at[len(loads)])
        copy.start()
        loads.append(copy)
        return copy

    load_g = load(g_hbm, rows.at[tp, 0])
    load_x = load(x_hbm, rows.at[tp, 1])
    load_s = [load(s_hbm.at[:, pl.ds(i * half, half)], own_s.at[i]) for i in range(2)]
    load_wo = [load(wo_hbm.at[:, pl.ds(i * half, half)], wo_v.at[i]) for i in range(2)]
    load_wi = [load(wi_hbm.at[:, pl.ds(i * half, half)], wi_v.at[i]) for i in range(2)]

    barrier = pltpu.get_barrier_semaphore()
    for peer in peers:
        pl.semaphore_signal(barrier, inc=1, device_id=peer, device_id_type=pl.DeviceIdType.MESH)
    pl.semaphore_wait(barrier, len(peers))

    sends = []
    pending = {}

    def send(src, dst, recv_sem, peer):
        pending[(id(recv_sem[0]), recv_sem[1:])] = (dst, recv_sem)
        recv_sem = recv_sem[0].at[recv_sem[1:]]
        copy = pltpu.make_async_remote_copy(
            src_ref=src, dst_ref=dst, send_sem=send_sem.at[len(sends)], recv_sem=recv_sem,
            device_id=peer, device_id_type=pl.DeviceIdType.MESH,
        )
        copy.start()
        sends.append(copy)

    def arrived(dst, recv_sem):
        pending.pop((id(recv_sem[0]), recv_sem[1:]))
        recv_sem = recv_sem[0].at[recv_sem[1:]]
        pltpu.make_async_remote_copy(
            src_ref=dst, dst_ref=dst, send_sem=send_sem.at[0], recv_sem=recv_sem,
            device_id=partner, device_id_type=pl.DeviceIdType.MESH,
        ).wait_recv()

    slot = lambda x_, h_: x_ * nh + h_
    h_left, h_right, h_far = lax.rem(h + nh - 1, nh), lax.rem(h + 1, nh), lax.rem(h + 2, nh)

    def to_x(which, h_):
        block = rows.at[slot(x, h_)]
        for k in range(1, nx):
            send(block, block, (ax_sem, k - 1, which), x_peer[k])

    load_g.wait()
    load_x.wait()
    mine = rows.at[tp]
    send(mine, mine, (az_sem, 0), right)
    send(mine, mine, (az_sem, 1), left)

    for copy in load_s:
        copy.wait()
    send(own_s.at[other], peer_s, (s_sem, 0), partner)
    to_x(0, h)

    arrived(peer_s, (s_sem, 0))
    own, peer = gelu_parts(own_s[core]), gelu_parts(peer_s[...])
    n = own[0].shape[0]
    first = core == 0
    for ref, i in ((quad, 0), (slope, 1)):
        ref[0:n, :] = jnp.where(first, own[i], peer[i])
        ref[n : 2 * n, :] = jnp.where(first, peer[i], own[i])
    hid[core, y, z] = quad[...].astype(bf16)

    def to_z(buf, sem):
        block = buf.at[core, y, z]
        for k in range(1, nz):
            send(block, block, (sem, k - 1), z_peer[k])

    def from_z(buf, sem):
        for k in range(1, nz):
            arrived(buf.at[core, y, lax.rem(z + nz - k, nz)], (sem, k - 1))

    def to_y(buf, sem):
        block = buf.at[core, y]
        for k in range(1, ny):
            send(block, block, (sem, k - 1), y_peer[k])

    def from_y(buf, sem, k):
        arrived(buf.at[core, lax.rem(y + ny - k, ny)], (sem, k - 1))

    from_left = rows.at[slot(x, h_left)]
    arrived(from_left, (az_sem, 0))
    send(from_left, from_left, (az_sem, 2), right)
    to_x(1, h_left)
    arrived(rows.at[slot(x, h_right)], (az_sem, 1))
    to_x(2, h_right)
    near, step = nh - 1, rows.shape[2]
    groups = (h, h_left, h_right, h_far)

    def from_x(which):
        for k in range(1, nx):
            arrived(rows.at[slot(lax.rem(x + nx - k, nx), groups[which])], (ax_sem, k - 1, which))

    def product(lo, hi):
        count = (hi - lo) * nx
        for g in range(lo, hi):
            for x_ in range(nx):
                r = ((g - lo) * nx + x_) * step
                wide[r : r + step, :] = rows[slot(x_, groups[g]), 0].astype(f32)
        lhs = wide[0 : count * step, :].astype(bf16)

        def place(ref, which):
            out = jnp.dot(lhs, wo_v[which], preferred_element_type=f32).reshape(count, step, half)
            for g in range(lo, hi):
                for x_ in range(nx):
                    ref[x_, g] = out[(g - lo) * nx + x_].astype(ref.dtype)

        place(b1_send, other)
        for k in order:
            y_ = lax.rem(y + k, ny)
            send(b1_send.at[y_, lo:hi], b1_recv.at[y_, lo:hi], (b1_sem, k, lo), partner)
        place(b1_own, core)

    def fold(lo, hi):
        for k in order:
            y_ = lax.rem(y + k, ny)
            arrived(b1_recv.at[y_, lo:hi], (b1_sem, k, lo))
            total = b1_own[y_, lo:hi] + b1_recv[y_, lo:hi].astype(f32)
            if k:
                b2_send[k - 1, lo:hi] = total.astype(bf16)
                send(b2_send.at[k - 1, lo:hi], b2_recv.at[k - 1, lo:hi], (b2_sem, k - 1, lo), y_peer[k])
            else:
                b2_sum[lo:hi] = total

    order = list(range(1, ny)) + [0]
    for which in range(near):
        from_x(which)
    for copy in load_wo:
        copy.wait()
    product(0, near)
    fold(0, near)
    arrived(rows.at[slot(x, h_far)], (az_sem, 2))
    to_x(near, h_far)
    from_x(near)
    product(near, nh)
    fold(near, nh)
    to_z(hid, hz_sem)
    for lo, hi in ((0, near), (near, nh)):
        for k in range(1, ny):
            arrived(b2_recv.at[k - 1, lo:hi], (b2_sem, k - 1, lo))
        for g in range(lo, hi):
            total = b2_sum[g]
            for k in range(1, ny):
                total = total + b2_recv[k - 1, g].astype(f32)
            b2_rows[pl.ds(pl.multiple_of(groups[g] * step, step), step), :] = total
    deep = b3_own.shape[1]
    for j in range(nz):
        piece = b2_rows[j * deep : (j + 1) * deep, :]
        b3_own[j] = piece
        b3_send[j] = piece.astype(bf16)
    for k in range(1, nz):
        send(b3_send.at[lax.rem(z + k, nz)], b3_recv.at[k - 1], (b3_sem, k - 1), z_peer[k])
    from_z(hid, hz_sem)
    to_y(hid, hy_sem)
    total = b3_own[z]
    for k in range(1, nz):
        arrived(b3_recv.at[k - 1], (b3_sem, k - 1))
        total = total + b3_recv[k - 1].astype(f32)
    pre[core, y, z] = (total * slope[...]).astype(bf16)
    def gathered(which, out):
        for t in range(rows.shape[0]):
            wide[t * step : (t + 1) * step, :] = rows[t, which].astype(f32)
        out[...] = wide[...].astype(bf16)

    to_z(pre, c1_sem)
    gathered(0, grad_rows)
    gathered(1, input_rows)
    from_z(pre, c1_sem)
    to_y(pre, c2_sem)
    send(pre.at[core, y], pre.at[core, y], (c3_sem, 0), partner)
    for k in range(1, ny):
        from_y(pre, c2_sem, k)
        block = pre.at[core, lax.rem(y + ny - k, ny)]
        send(block, block, (c3_sem, k), partner)

    for k in range(1, ny):
        from_y(hid, hy_sem, k)
    send(hid.at[core], hid.at[core], (hc_sem, 0), partner)

    def packed(buf, which, out):
        for i in range(ny):
            for j in range(nz):
                r = (i * nz + j) * deep
                pack[r : r + deep, :] = buf[which, i, j].astype(f32)
        out[which] = pack[...].astype(bf16)

    def back(which):
        return lax.dot_general(
            pre_full[which], wi_v[which], (((1,), (1,)), ((), ())), preferred_element_type=f32
        )

    for copy in load_wi:
        copy.wait()
    packed(pre, core, pre_full)
    part = back(core)
    for k in range(ny):
        arrived(pre.at[other, lax.rem(y + ny - k, ny)], (c3_sem, k))
    packed(pre, other, pre_full)
    part = part + back(other)
    dx_part[...] = part.reshape(dx_part.shape)
    for k in range(1, nx):
        dx_send[k - 1] = dx_part[lax.rem(x + k, nx)].astype(bf16)
        send(dx_send.at[k - 1], dx_recv.at[k - 1], (dx_sem, k - 1), x_peer[k])
    arrived(hid.at[other], (hc_sem, 0))
    packed(hid, 0, hid_full)
    packed(hid, 1, hid_full)
    total = dx_part[x]
    for k in range(1, nx):
        arrived(dx_recv.at[k - 1], (dx_sem, k - 1))
        total = total + dx_recv[k - 1].astype(f32)
    dz_part[...] = total.reshape(dz_part.shape)
    dz_send[0] = dz_part[h_far].astype(bf16)
    dz_send[1] = dz_part[h_left].astype(bf16)
    send(dz_send.at[0], dz_recv.at[0], (dz_sem, 0), right)
    send(dz_send.at[1], dz_recv.at[1], (dz_sem, 1), left)

    def outer(a, b):
        return lax.dot_general(
            a[...], b, (((0,), (0,)), ((), ())), preferred_element_type=f32
        ).astype(bf16)

    for i in range(2):
        gwi_v[:, i * half : (i + 1) * half] = outer(input_rows, pre_full[i])
    arrived(dz_recv.at[0], (dz_sem, 0))
    dz_send[2] = (dz_part[h_right] + dz_recv[0].astype(f32)).astype(bf16)
    send(dz_send.at[2], dz_recv.at[2], (dz_sem, 2), right)
    for i in range(2):
        gwo_v[:, i * half : (i + 1) * half] = outer(grad_rows, hid_full[i])
    arrived(dz_recv.at[1], (dz_sem, 1))
    arrived(dz_recv.at[2], (dz_sem, 2))
    gin_v[...] = (dz_part[h] + dz_recv[1].astype(f32) + dz_recv[2].astype(f32)).astype(bf16)
    for copy in sends:
        copy.wait_send()


def put(*refs):
    sems = refs[6]
    copies = [pltpu.make_async_copy(refs[i], refs[3 + i], sems.at[i]) for i in range(3)]
    for copy in copies:
        copy.start()
    for copy in copies:
        copy.wait()


def on_device(inputs, grad_out, saved_pre, w_in, w_out):
    ny, nz, nx, nh = (GRID[k] for k in ("ny", "nz", "nx", "nh"))
    step, width = inputs.shape
    n, hidden = saved_pre.shape
    half = hidden // 2
    tokens = step * nx * nh
    deep = tokens // (ny * nz)
    per_y, per_x = tokens // ny, tokens // nx
    vmem, dma = pltpu.VMEM, pltpu.SemaphoreType.DMA
    shapes = ((step, width), (width, hidden), (width, hidden))
    any_space = pl.BlockSpec(memory_space=pl.ANY)
    n_sends = ny + ny - 1 + 3 + 4 * (nx - 1) + 1 + 3 * (nz - 1) + 3 * (ny - 1) + ny + 1 + ny + (nx - 1) + 3
    results = pl.pallas_call(
        functools.partial(kernel, ny, nz, nx, nh),
        out_shape=tuple(vmem(shape, bf16) for shape in shapes),
        in_specs=[any_space] * 5,
        out_specs=(pl.BlockSpec(memory_space=vmem),) * 3,
        scratch_shapes=[
            vmem((nx * nh, 2, step, width), bf16),
            vmem((2, n, half), bf16),
            vmem((n, half), bf16),
            vmem((2, width, half), bf16),
            vmem((2, width, half), bf16),
            vmem((tokens, width), f32),
            vmem((tokens, width), bf16),
            vmem((tokens, width), bf16),
            vmem((deep, half), f32),
            vmem((deep, half), f32),
            vmem((2, ny, nz, deep, half), bf16),
            vmem((2, ny, nz, deep, half), bf16),
            vmem((ny, nh, step, half), bf16),
            vmem((ny, nh, step, half), bf16),
            vmem((ny, nh, step, half), f32),
            vmem((ny - 1, nh, step, half), bf16),
            vmem((ny - 1, nh, step, half), bf16),
            vmem((nh, step, half), f32),
            vmem((per_y, half), f32),
            vmem((nz, deep, half), bf16),
            vmem((nz, deep, half), f32),
            vmem((nz - 1, deep, half), bf16),
            vmem((tokens, half), f32),
            vmem((2, tokens, half), bf16),
            vmem((2, tokens, half), bf16),
            vmem((nx, per_x, width), f32),
            vmem((nx - 1, per_x, width), bf16),
            vmem((nx - 1, per_x, width), bf16),
            vmem((nh, step, width), f32),
            vmem((3, step, width), bf16),
            vmem((3, step, width), bf16),
            dma((11,)),
            dma((n_sends,)),
            dma((3,)),
            dma((nx - 1, 4)),
            dma((1,)),
            dma((nz - 1,)),
            dma((ny - 1,)),
            dma((1,)),
            dma((ny, nh)),
            dma((ny - 1, nh)),
            dma((nz - 1,)),
            dma((nz - 1,)),
            dma((ny - 1,)),
            dma((ny,)),
            dma((nx - 1,)),
            dma((3,)),
        ],
        compiler_params=pltpu.CompilerParams(
            collective_id=0, has_side_effects=True
        ),
    )(inputs, grad_out, saved_pre, w_in, w_out.T)
    grad_in, grad_w_in, grad_w_out = pl.pallas_call(
        put,
        out_shape=tuple(jax.ShapeDtypeStruct(shape, bf16) for shape in shapes),
        in_specs=[pl.BlockSpec(memory_space=vmem)] * 3,
        out_specs=(any_space,) * 3,
        scratch_shapes=[dma((3,))],
    )(*[pltpu.with_memory_space_constraint(r, vmem) for r in results])
    return grad_in, grad_w_in, grad_w_out.T


def solution(mesh):
    return jax.shard_map(
        on_device,
        mesh=mesh,
        in_specs=(
            P("tensor", "dp"),
            P("tensor", "dp"),
            P("dp", "tensor"),
            P("dp", "tensor"),
            P("tensor", "dp"),
        ),
        out_specs=(P("tensor", "dp"), P("dp", "tensor"), P("tensor", "dp")),
        check_vma=False,
    )
```

```python
import functools

import jax
import jax.numpy as jnp
from jax import lax
from jax.experimental import pallas as pl
from jax.experimental.pallas import tpu as pltpu
from jax.sharding import PartitionSpec as P

GRID = dict(ny=4, nz=8, nx=4, nh=4)

root_half = 0.7071067811865476
inv_root_two_pi = 0.3989422804014327
bf16, f32 = jnp.bfloat16, jnp.float32


def gelu_parts(saved):
    value = saved.astype(f32)
    cdf = 0.5 * (1.0 + lax.erf(value * root_half))
    density = inv_root_two_pi * jnp.exp(-0.5 * value * value)
    return value * cdf, cdf + value * density


def kernel(
    ny, nz, nx, nh,
    x_hbm, g_hbm, s_hbm, wi_hbm, wo_hbm,
    gin_v, gwi_v, gwo_v,
    rows, own_s, peer_s, wi_v, wo_v, wide, grad_rows, input_rows,
    slope, quad, hid, pre,
    b1_send, b1_recv, b1_own, b2_send, b2_recv, b2_sum, b2_rows, b3_send, b3_own, b3_recv,
    pack, hid_full, pre_full,
    fx_part, fx_send, fx_recv, dx_part, dx_send, dx_recv, dz_part, dz_send, dz_recv,
    local_sem, send_sem,
    az_sem, ax_sem, s_sem, hz_sem, hy_sem, hc_sem,
    b1_sem, b2_sem, b3_sem, c1_sem, c2_sem, c3_sem, dx_sem, dz_sem,
):
    dp, tp = lax.axis_index("dp"), lax.axis_index("tensor")
    core = lax.rem(dp, 2)
    chip = lax.div(dp, 2)
    z, y = lax.rem(chip, nz), lax.div(chip, nz)
    x, h = lax.div(tp, nh), lax.rem(tp, nh)
    other = 1 - core

    def at(y=y, z=z, core=core, x=x, h=h):
        return {"dp": (y * nz + z) * 2 + core, "tensor": x * nh + h}

    y_peer = [None] + [at(y=lax.rem(y + k, ny)) for k in range(1, ny)]
    z_peer = [None] + [at(z=lax.rem(z + k, nz)) for k in range(1, nz)]
    x_peer = [None] + [at(x=lax.rem(x + k, nx)) for k in range(1, nx)]
    right, left = at(h=lax.rem(h + 1, nh)), at(h=lax.rem(h + nh - 1, nh))
    partner = at(core=other)
    peers = y_peer[1:] + z_peer[1:] + x_peer[1:] + [right, left, partner]

    half = wi_v.shape[2]

    def load(src, dst, i):
        copy = pltpu.make_async_copy(src, dst, local_sem.at[i])
        copy.start()
        return copy

    load_g = load(g_hbm, rows.at[tp, 0], 0)
    load_x = load(x_hbm, rows.at[tp, 1], 1)
    for i in range(2):
        columns = pl.ds(i * half, half)
        for hbm, ref, sem in ((s_hbm, own_s, 2), (wo_hbm, wo_v, 3), (wi_hbm, wi_v, 4)):
            load(hbm.at[:, columns], ref.at[i], sem)

    def loaded(ref, sem):
        pltpu.make_async_copy(ref, ref, local_sem.at[sem]).wait()

    barrier = pltpu.get_barrier_semaphore()
    for peer in peers:
        pl.semaphore_signal(barrier, inc=1, device_id=peer, device_id_type=pl.DeviceIdType.MESH)
    pl.semaphore_wait(barrier, len(peers))

    def send(src, dst, group, recv_sem, peer):
        pltpu.make_async_remote_copy(
            src_ref=src, dst_ref=dst, send_sem=send_sem.at[group], recv_sem=recv_sem,
            device_id=peer, device_id_type=pl.DeviceIdType.MESH,
        ).start()

    def handle(ref, group, recv_sem):
        return pltpu.make_async_remote_copy(
            src_ref=ref, dst_ref=ref, send_sem=send_sem.at[group], recv_sem=recv_sem,
            device_id=partner, device_id_type=pl.DeviceIdType.MESH,
        )

    def arrived(ref, recv_sem):
        handle(ref, 0, recv_sem).wait_recv()

    slot = lambda x_, h_: x_ * nh + h_
    h_left, h_right, h_far = lax.rem(h + nh - 1, nh), lax.rem(h + 1, nh), lax.rem(h + 2, nh)

    def to_x(which, h_):
        block = rows.at[slot(x, h_)]
        for k in range(1, nx):
            send(block, block, 0, ax_sem.at[0 if which < nh - 1 else 1], x_peer[k])

    load_g.wait()
    load_x.wait()
    mine = rows.at[tp]
    send(mine, mine, 0, az_sem.at[0], right)
    send(mine, mine, 0, az_sem.at[1], left)

    loaded(own_s, 2)
    send(own_s.at[other], peer_s, 1, s_sem.at[0], partner)
    to_x(0, h)

    arrived(peer_s, s_sem.at[0])
    own, peer = gelu_parts(own_s[core]), gelu_parts(peer_s[...])
    n = own[0].shape[0]
    first = core == 0
    for ref, i in ((quad, 0), (slope, 1)):
        ref[0:n, :] = jnp.where(first, own[i], peer[i])
        ref[n : 2 * n, :] = jnp.where(first, peer[i], own[i])
    hid[core, y, z] = quad[...].astype(bf16)

    def to_z(buf, group, sem):
        block = buf.at[core, y, z]
        for k in range(1, nz):
            send(block, block, group, sem.at[0], z_peer[k])

    def from_z(buf, sem):
        arrived(buf.at[core, y, 0 : nz - 1], sem.at[0])

    from_left = rows.at[slot(x, h_left)]
    arrived(from_left, az_sem.at[0])
    send(from_left, from_left, 0, az_sem.at[2], right)
    to_x(1, h_left)
    arrived(rows.at[slot(x, h_right)], az_sem.at[1])
    to_x(2, h_right)
    near, step = nh - 1, rows.shape[2]
    groups = (h, h_left, h_right, h_far)

    def product(lo, hi):
        count = (hi - lo) * nx
        for g in range(lo, hi):
            for x_ in range(nx):
                r = ((g - lo) * nx + x_) * step
                wide[r : r + step, :] = rows[slot(x_, groups[g]), 0].astype(f32)
        lhs = wide[0 : count * step, :].astype(bf16)

        def place(ref, which):
            out = jnp.dot(lhs, wo_v[which], preferred_element_type=f32).reshape(count, step, half)
            for g in range(lo, hi):
                for x_ in range(nx):
                    ref[x_, g] = out[(g - lo) * nx + x_].astype(ref.dtype)

        place(b1_send, other)
        for k in order:
            y_ = lax.rem(y + k, ny)
            send(b1_send.at[y_, lo:hi], b1_recv.at[y_, lo:hi], 2, b1_sem.at[ny if lo else k], partner)
        place(b1_own, core)

    def fold(lo, hi):
        if lo:
            arrived(b1_recv.at[:, lo:hi], b1_sem.at[ny])
        for k in order:
            y_ = lax.rem(y + k, ny)
            if lo == 0:
                arrived(b1_recv.at[y_, lo:hi], b1_sem.at[k])
            total = b1_own[y_, lo:hi] + b1_recv[y_, lo:hi].astype(f32)
            if k:
                b2_send[k - 1, lo:hi] = total.astype(bf16)
                send(b2_send.at[k - 1, lo:hi], b2_recv.at[k - 1, lo:hi], 3, b2_sem.at[1 if lo else 0], y_peer[k])
            else:
                b2_sum[lo:hi] = total

    order = list(range(1, ny)) + [0]
    arrived(rows.at[0 : near * (nx - 1)], ax_sem.at[0])
    loaded(wo_v, 3)
    product(0, near)
    fold(0, near)
    arrived(rows.at[slot(x, h_far)], az_sem.at[2])
    to_x(near, h_far)
    arrived(rows.at[0 : nx - 1], ax_sem.at[1])
    product(near, nh)
    fold(near, nh)
    to_z(hid, 5, hz_sem)
    for lo, hi in ((0, near), (near, nh)):
        arrived(b2_recv.at[:, lo:hi], b2_sem.at[1 if lo else 0])
        for g in range(lo, hi):
            total = b2_sum[g]
            for k in range(1, ny):
                total = total + b2_recv[k - 1, g].astype(f32)
            b2_rows[pl.ds(pl.multiple_of(groups[g] * step, step), step), :] = total
    deep = b3_own.shape[1]
    for j in range(nz):
        piece = b2_rows[j * deep : (j + 1) * deep, :]
        b3_own[j] = piece
        b3_send[j] = piece.astype(bf16)
    for k in range(1, nz):
        send(b3_send.at[lax.rem(z + k, nz)], b3_recv.at[k - 1], 4, b3_sem.at[0], z_peer[k])
    from_z(hid, hz_sem)
    for k in range(1, ny):
        send(hid.at[core, y], hid.at[core, y], 7, hy_sem.at[0], y_peer[k])
    total = b3_own[z]
    arrived(b3_recv, b3_sem.at[0])
    for k in range(1, nz):
        total = total + b3_recv[k - 1].astype(f32)
    pre[core, y, z] = (total * slope[...]).astype(bf16)
    def gathered(which, out):
        for t in range(rows.shape[0]):
            wide[t * step : (t + 1) * step, :] = rows[t, which].astype(f32)
        out[...] = wide[...].astype(bf16)

    to_z(pre, 6, c1_sem)
    gathered(0, grad_rows)
    gathered(1, input_rows)
    from_z(pre, c1_sem)
    per = step // deep
    far_first = (near,) + tuple(range(near))

    def part_of(half_, y_, g):
        return pre.at[half_, y_, pl.ds(groups[g] * per, per)]

    def y_back(k):
        return lax.rem(y + ny - k, ny)

    for g in far_first:
        block = part_of(core, y, g)
        for k in range(1, ny):
            send(block, block, 9, c2_sem.at[k - 1 if g == near else ny - 1], y_peer[k])
        send(block, block, 10, c3_sem.at[0 if g == near else 1], partner)

    def packed(buf, which, out):
        for i in range(ny):
            for j in range(nz):
                r = (i * nz + j) * deep
                pack[r : r + deep, :] = buf[which, i, j].astype(f32)
        out[which] = pack[...].astype(bf16)

    def back(lhs, which):
        return lax.dot_general(lhs, wi_v[which], (((1,), (1,)), ((), ())), preferred_element_type=f32)

    def far_back(which):
        for i in range(ny):
            for j in range(per):
                r = i * step + j * deep
                pack[r : r + deep, :] = pre[which, i, h_far * per + j].astype(f32)
        return back(pack[0 : ny * step, :].astype(bf16), which)

    for k in range(1, ny):
        block = part_of(core, y_back(k), near)
        arrived(block, c2_sem.at[k - 1])
        send(block, block, 10, c3_sem.at[0], partner)
    loaded(wi_v, 4)
    part = far_back(core)
    arrived(pre.at[other, :, 0:per], c3_sem.at[0])
    part = part + far_back(other)

    fx_part[...] = part.reshape(fx_part.shape)
    for k in range(1, nx):
        fx_send[k - 1] = fx_part[lax.rem(x + k, nx)].astype(bf16)
        send(fx_send.at[k - 1], fx_recv.at[k - 1], 11, dx_sem.at[1], x_peer[k])
    arrived(pre.at[core, 0 : ny - 1, 0 : near * per], c2_sem.at[ny - 1])
    for g in range(near):
        for k in range(1, ny):
            block = part_of(core, y_back(k), g)
            send(block, block, 10, c3_sem.at[1], partner)
    arrived(hid.at[core, 0 : ny - 1], hy_sem.at[0])
    send(hid.at[core], hid.at[core], 8, hc_sem.at[0], partner)
    total = fx_part[x]
    arrived(fx_recv, dx_sem.at[1])
    for k in range(1, nx):
        total = total + fx_recv[k - 1].astype(f32)
    dz_send[0] = total.astype(bf16)
    send(dz_send.at[0], dz_recv.at[0], 13, dz_sem.at[0], right)
    packed(pre, core, pre_full)
    part = back(pre_full[core], core)
    arrived(pre.at[other, :, 0 : near * per], c3_sem.at[1])
    packed(pre, other, pre_full)
    part = part + back(pre_full[other], other)
    dx_part[...] = part.reshape(dx_part.shape)
    for k in range(1, nx):
        for g in range(near):
            dx_send[k - 1, g] = dx_part[lax.rem(x + k, nx), groups[g]].astype(bf16)
        send(dx_send.at[k - 1], dx_recv.at[k - 1], 12, dx_sem.at[0], x_peer[k])
    arrived(dx_recv, dx_sem.at[0])
    for g in range(near):
        total = dx_part[x, groups[g]]
        for k in range(1, nx):
            total = total + dx_recv[k - 1, g].astype(f32)
        dz_part[g] = total
    dz_send[1] = dz_part[1].astype(bf16)
    send(dz_send.at[1], dz_recv.at[1], 13, dz_sem.at[1], left)
    arrived(dz_recv.at[0], dz_sem.at[0])
    dz_send[2] = (dz_part[2] + dz_recv[0].astype(f32)).astype(bf16)
    send(dz_send.at[2], dz_recv.at[2], 13, dz_sem.at[2], right)

    def outer(a, b):
        return lax.dot_general(
            a[...], b, (((0,), (0,)), ((), ())), preferred_element_type=f32
        ).astype(bf16)

    for i in range(2):
        gwi_v[:, i * half : (i + 1) * half] = outer(input_rows, pre_full[i])
    arrived(hid.at[other], hc_sem.at[0])
    for i in range(2):
        packed(hid, i, hid_full)
        gwo_v[:, i * half : (i + 1) * half] = outer(grad_rows, hid_full[i])
    arrived(dz_recv.at[1], dz_sem.at[1])
    arrived(dz_recv.at[2], dz_sem.at[2])
    gin_v[...] = (dz_part[0] + dz_recv[1].astype(f32) + dz_recv[2].astype(f32)).astype(bf16)
    sent = (
        rows.at[0 : 3 + nh * (nx - 1)], peer_s, b1_send, b2_send, b3_send.at[0 : nz - 1],
        hid.at[core, y, 0 : nz - 1], pre.at[core, y, 0 : nz - 1], hid.at[core, 0 : ny - 1],
        hid.at[core], pre.at[core, 0 : ny - 1], pre.at[core], fx_send, dx_send, dz_send,
    )
    for group, ref in enumerate(sent):
        handle(ref, group, s_sem.at[0]).wait_send()


def put(*refs):
    sems = refs[6]
    copies = [pltpu.make_async_copy(refs[i], refs[3 + i], sems.at[i]) for i in range(3)]
    for copy in copies:
        copy.start()
    for copy in copies:
        copy.wait()


def on_device(inputs, grad_out, saved_pre, w_in, w_out):
    ny, nz, nx, nh = (GRID[k] for k in ("ny", "nz", "nx", "nh"))
    step, width = inputs.shape
    n, hidden = saved_pre.shape
    half = hidden // 2
    tokens = step * nx * nh
    deep = tokens // (ny * nz)
    per_y = tokens // ny
    vmem, dma = pltpu.VMEM, pltpu.SemaphoreType.DMA
    shapes = ((step, width), (width, hidden), (width, hidden))
    any_space = pl.BlockSpec(memory_space=pl.ANY)
    results = pl.pallas_call(
        functools.partial(kernel, ny, nz, nx, nh),
        out_shape=tuple(vmem(shape, bf16) for shape in shapes),
        in_specs=[any_space] * 5,
        out_specs=(pl.BlockSpec(memory_space=vmem),) * 3,
        scratch_shapes=[
            vmem((nx * nh, 2, step, width), bf16),
            vmem((2, n, half), bf16),
            vmem((n, half), bf16),
            vmem((2, width, half), bf16),
            vmem((2, width, half), bf16),
            vmem((tokens, width), f32),
            vmem((tokens, width), bf16),
            vmem((tokens, width), bf16),
            vmem((deep, half), f32),
            vmem((deep, half), f32),
            vmem((2, ny, nz, deep, half), bf16),
            vmem((2, ny, nz, deep, half), bf16),
            vmem((ny, nh, step, half), bf16),
            vmem((ny, nh, step, half), bf16),
            vmem((ny, nh, step, half), f32),
            vmem((ny - 1, nh, step, half), bf16),
            vmem((ny - 1, nh, step, half), bf16),
            vmem((nh, step, half), f32),
            vmem((per_y, half), f32),
            vmem((nz, deep, half), bf16),
            vmem((nz, deep, half), f32),
            vmem((nz - 1, deep, half), bf16),
            vmem((tokens, half), f32),
            vmem((2, tokens, half), bf16),
            vmem((2, tokens, half), bf16),
            vmem((nx, step, width), f32),
            vmem((nx - 1, step, width), bf16),
            vmem((nx - 1, step, width), bf16),
            vmem((nx, nh, step, width), f32),
            vmem((nx - 1, nh - 1, step, width), bf16),
            vmem((nx - 1, nh - 1, step, width), bf16),
            vmem((nh - 1, step, width), f32),
            vmem((3, step, width), bf16),
            vmem((3, step, width), bf16),
            dma((5,)),
            dma((14,)),
            dma((3,)),
            dma((2,)),
            dma((1,)),
            dma((1,)),
            dma((1,)),
            dma((1,)),
            dma((ny + 1,)),
            dma((2,)),
            dma((1,)),
            dma((1,)),
            dma((ny,)),
            dma((2,)),
            dma((2,)),
            dma((3,)),
        ],
        compiler_params=pltpu.CompilerParams(
            collective_id=0, has_side_effects=True
        ),
    )(inputs, grad_out, saved_pre, w_in, w_out.T)
    grad_in, grad_w_in, grad_w_out = pl.pallas_call(
        put,
        out_shape=tuple(jax.ShapeDtypeStruct(shape, bf16) for shape in shapes),
        in_specs=[pl.BlockSpec(memory_space=vmem)] * 3,
        out_specs=(any_space,) * 3,
        scratch_shapes=[dma((3,))],
    )(*[pltpu.with_memory_space_constraint(r, vmem) for r in results])
    return grad_in, grad_w_in, grad_w_out.T


def solution(mesh):
    return jax.shard_map(
        on_device,
        mesh=mesh,
        in_specs=(
            P("tensor", "dp"),
            P("tensor", "dp"),
            P("dp", "tensor"),
            P("dp", "tensor"),
            P("tensor", "dp"),
        ),
        out_specs=(P("tensor", "dp"), P("dp", "tensor"), P("tensor", "dp")),
        check_vma=False,
    )
```

```python
import functools

import jax
import jax.numpy as jnp
from jax import lax
from jax.experimental import pallas as pl
from jax.experimental.pallas import tpu as pltpu
from jax.sharding import PartitionSpec as P

GRID = dict(ny=4, nz=8, nx=4, nh=4)

root_half = 0.7071067811865476
inv_root_two_pi = 0.3989422804014327
bf16, f32 = jnp.bfloat16, jnp.float32


def gelu_parts(saved):
    value = saved.astype(f32)
    cdf = 0.5 * (1.0 + lax.erf(value * root_half))
    density = inv_root_two_pi * jnp.exp(-0.5 * value * value)
    return value * cdf, cdf + value * density


def kernel(
    ny, nz, nx, nh,
    x_hbm, g_hbm, s_hbm, wi_hbm, wo_hbm,
    gin_v, gwi_v, gwo_v,
    rows, own_s, peer_s, wi_v, wo_v, wide, grad_rows, input_rows,
    slope, quad, saved_send, saved_recv, hid, pre,
    b1_send, b1_recv, b1_own, b2_send, b2_recv, b2_sum, b3_send, b3_own, b3_recv,
    pack, hid_full, pre_full,
    fx_part, fx_send, fx_recv, dx_part, dx_send, dx_recv, dz_part, dz_send, dz_recv,
    local_sem, send_sem,
    az_sem, ax_sem, s_sem, sv_sem, hz_sem, hy_sem, hc_sem,
    b1_sem, b2_sem, b3_sem, c1_sem, c2_sem, c3_sem, dx_sem, dz_sem,
):
    dp, tp = lax.axis_index("dp"), lax.axis_index("tensor")
    core = lax.rem(dp, 2)
    chip = lax.div(dp, 2)
    z, y = lax.rem(chip, nz), lax.div(chip, nz)
    x, h = lax.div(tp, nh), lax.rem(tp, nh)
    other = 1 - core

    def at(y=y, z=z, core=core, x=x, h=h):
        return {"dp": (y * nz + z) * 2 + core, "tensor": x * nh + h}

    y_peer = [None] + [at(y=lax.rem(y + k, ny)) for k in range(1, ny)]
    z_peer = [None] + [at(z=lax.rem(z + k, nz)) for k in range(1, nz)]
    x_peer = [None] + [at(x=lax.rem(x + k, nx)) for k in range(1, nx)]
    right, left = at(h=lax.rem(h + 1, nh)), at(h=lax.rem(h + nh - 1, nh))
    partner = at(core=other)
    peers = y_peer[1:] + z_peer[1:] + x_peer[1:] + [right, left, partner]

    half = wi_v.shape[2]

    def load(src, dst, i):
        copy = pltpu.make_async_copy(src, dst, local_sem.at[i])
        copy.start()
        return copy

    load_g = load(g_hbm, rows.at[tp, 0], 0)
    load_x = load(x_hbm, rows.at[tp, 1], 1)
    for i in range(2):
        columns = pl.ds(i * half, half)
        for hbm, ref, sem in ((s_hbm, own_s, 2), (wo_hbm, wo_v, 3), (wi_hbm, wi_v, 4)):
            load(hbm.at[:, columns], ref.at[i], sem)

    def loaded(ref, sem):
        pltpu.make_async_copy(ref, ref, local_sem.at[sem]).wait()

    barrier = pltpu.get_barrier_semaphore()
    for peer in peers:
        pl.semaphore_signal(barrier, inc=1, device_id=peer, device_id_type=pl.DeviceIdType.MESH)
    pl.semaphore_wait(barrier, len(peers))

    def send(src, dst, group, recv_sem, peer):
        pltpu.make_async_remote_copy(
            src_ref=src, dst_ref=dst, send_sem=send_sem.at[group], recv_sem=recv_sem,
            device_id=peer, device_id_type=pl.DeviceIdType.MESH,
        ).start()

    def handle(ref, group, recv_sem):
        return pltpu.make_async_remote_copy(
            src_ref=ref, dst_ref=ref, send_sem=send_sem.at[group], recv_sem=recv_sem,
            device_id=partner, device_id_type=pl.DeviceIdType.MESH,
        )

    def arrived(ref, recv_sem):
        handle(ref, 0, recv_sem).wait_recv()

    slot = lambda x_, h_: x_ * nh + h_
    h_left, h_right, h_far = lax.rem(h + nh - 1, nh), lax.rem(h + 1, nh), lax.rem(h + 2, nh)

    def to_x(which, h_):
        block = rows.at[slot(x, h_)]
        for k in range(1, nx):
            send(block, block, 0, ax_sem.at[0 if which < nh - 1 else 1], x_peer[k])

    load_g.wait()
    load_x.wait()
    mine = rows.at[tp]
    send(mine, mine, 0, az_sem.at[0], right)
    send(mine, mine, 0, az_sem.at[1], left)

    loaded(own_s, 2)
    send(own_s.at[other], peer_s, 1, s_sem.at[0], partner)
    to_x(0, h)

    arrived(peer_s, s_sem.at[0])
    step, deep = rows.shape[2], b3_own.shape[1]
    per = step // deep
    shift = lax.rem(nz // 2 - 1 - per * h_far + nz, nz)
    middle = [nz // 2 - 1 + i for i in range(per)]
    outside = [i for i in range(nz) if i not in middle]

    def piece_of(z_):
        return lax.rem(z_ + nz - shift, nz)

    own, peer = own_s[core].astype(f32), peer_s[...].astype(f32)
    n = own.shape[0]
    first = core == 0
    quad[0:n, :] = jnp.where(first, own, peer)
    quad[n : 2 * n, :] = jnp.where(first, peer, own)
    saved_send[...] = quad[...].astype(bf16)
    send(saved_send, saved_recv, 14, sv_sem.at[0], at(z=lax.rem(z + shift, nz)))
    hid[core, y, z] = gelu_parts(quad[...])[0].astype(bf16)

    def to_z(block, group, sem):
        for k in sorted(range(1, nz), key=lambda k: abs(2 * k - nz)):
            send(block, block, group, sem, z_peer[k])

    def from_z(buf, sem):
        arrived(buf.at[core, y, 0 : nz - 1], sem.at[0])

    from_left = rows.at[slot(x, h_left)]
    arrived(from_left, az_sem.at[0])
    send(from_left, from_left, 0, az_sem.at[2], right)
    to_x(1, h_left)
    arrived(rows.at[slot(x, h_right)], az_sem.at[1])
    to_x(2, h_right)
    near = nh - 1
    groups = (h, h_left, h_right, h_far)

    def product(lo, hi):
        count = (hi - lo) * nx
        for g in range(lo, hi):
            for x_ in range(nx):
                r = ((g - lo) * nx + x_) * step
                wide[r : r + step, :] = rows[slot(x_, groups[g]), 0].astype(f32)
        lhs = wide[0 : count * step, :].astype(bf16)

        def place(ref, which):
            out = jnp.dot(lhs, wo_v[which], preferred_element_type=f32).reshape(count, step, half)
            for g in range(lo, hi):
                for x_ in range(nx):
                    ref[x_, g] = out[(g - lo) * nx + x_].astype(ref.dtype)

        place(b1_send, other)
        for k in order:
            y_ = lax.rem(y + k, ny)
            send(b1_send.at[y_, lo:hi], b1_recv.at[y_, lo:hi], 2, b1_sem.at[ny if lo else k], partner)
        place(b1_own, core)

    def fold(lo, hi):
        if lo:
            arrived(b1_recv.at[:, lo:hi], b1_sem.at[ny])
        for k in order:
            y_ = lax.rem(y + k, ny)
            if lo == 0:
                arrived(b1_recv.at[y_, lo:hi], b1_sem.at[k])
            total = b1_own[y_, lo:hi] + b1_recv[y_, lo:hi].astype(f32)
            if k:
                b2_send[k - 1, lo:hi] = total.astype(bf16)
                send(b2_send.at[k - 1, lo:hi], b2_recv.at[k - 1, lo:hi], 3, b2_sem.at[1 if lo else 0], y_peer[k])
            else:
                b2_sum[lo:hi] = total

    order = list(range(1, ny)) + [0]
    arrived(rows.at[0 : near * (nx - 1)], ax_sem.at[0])
    loaded(wo_v, 3)
    product(0, near)
    fold(0, near)
    arrived(rows.at[slot(x, h_far)], az_sem.at[2])
    to_x(near, h_far)
    to_z(hid.at[core, y, z], 5, hz_sem.at[0])
    arrived(rows.at[0 : nx - 1], ax_sem.at[1])
    product(near, nh)
    fold(near, nh)
    for lo, hi, owners in ((0, near, outside), (near, nh, middle)):
        arrived(b2_recv.at[:, lo:hi], b2_sem.at[1 if lo else 0])
        for g in range(lo, hi):
            total = b2_sum[g]
            for k in range(1, ny):
                total = total + b2_recv[k - 1, g].astype(f32)
            b2_sum[g] = total
            for i in range(per):
                piece = b2_sum[g, i * deep : (i + 1) * deep, :]
                b3_own[groups[g] * per + i] = piece
                b3_send[groups[g] * per + i] = piece.astype(bf16)
        for owner in owners:

            @pl.when(z != owner)
            def _():
                send(b3_send.at[piece_of(owner)], b3_recv.at[z], 4, b3_sem.at[0], at(z=owner))
    mine = piece_of(z)
    arrived(saved_recv, sv_sem.at[0])
    slope[...] = gelu_parts(saved_recv[...])[1]
    from_z(hid, hz_sem)
    for k in range(1, ny):
        send(hid.at[core, y], hid.at[core, y], 7, hy_sem.at[0], y_peer[k])
    total = b3_own[mine]
    arrived(b3_recv.at[0 : nz - 1], b3_sem.at[0])
    for k in range(1, nz):
        total = total + b3_recv[lax.rem(z + k, nz)].astype(f32)
    pre[core, y, mine] = (total * slope[...]).astype(bf16)
    def gathered(which, out):
        for t in range(rows.shape[0]):
            wide[t * step : (t + 1) * step, :] = rows[t, which].astype(f32)
        out[...] = wide[...].astype(bf16)

    to_z(pre.at[core, y, mine], 6, c1_sem.at[z])
    gathered(0, grad_rows)
    gathered(1, input_rows)

    def from_owners(owners):
        for owner in owners:

            @pl.when(z != owner)
            def _():
                arrived(pre.at[core, y, piece_of(owner)], c1_sem.at[owner])

    from_owners(middle)

    def part_of(half_, y_, g):
        return pre.at[half_, y_, pl.ds(groups[g] * per, per)]

    def y_back(k):
        return lax.rem(y + ny - k, ny)

    def to_y(g):
        block = part_of(core, y, g)
        for k in range(1, ny):
            send(block, block, 9, c2_sem.at[k - 1 if g == near else ny - 1], y_peer[k])
        send(block, block, 10, c3_sem.at[0 if g == near else 1], partner)

    to_y(near)
    arrived(hid.at[core, 0 : ny - 1], hy_sem.at[0])
    send(hid.at[core], hid.at[core], 8, hc_sem.at[0], partner)

    def packed(buf, which, out):
        for i in range(ny):
            for j in range(nz):
                r = (i * nz + j) * deep
                pack[r : r + deep, :] = buf[which, i, j].astype(f32)
        out[which] = pack[...].astype(bf16)

    def back(lhs, which):
        return lax.dot_general(lhs, wi_v[which], (((1,), (1,)), ((), ())), preferred_element_type=f32)

    def far_back(which):
        for i in range(ny):
            for j in range(per):
                r = i * step + j * deep
                pack[r : r + deep, :] = pre[which, i, h_far * per + j].astype(f32)
        return back(pack[0 : ny * step, :].astype(bf16), which)

    for k in range(1, ny):
        block = part_of(core, y_back(k), near)
        arrived(block, c2_sem.at[k - 1])
        send(block, block, 10, c3_sem.at[0], partner)
    from_owners(outside)
    for g in range(near):
        to_y(g)
    loaded(wi_v, 4)
    part = far_back(core)
    arrived(pre.at[other, :, 0:per], c3_sem.at[0])
    part = part + far_back(other)

    fx_part[...] = part.reshape(fx_part.shape)
    for k in range(1, nx):
        fx_send[k - 1] = fx_part[lax.rem(x + k, nx)].astype(bf16)
        send(fx_send.at[k - 1], fx_recv.at[k - 1], 11, dx_sem.at[1], x_peer[k])
    total = fx_part[x]
    arrived(fx_recv, dx_sem.at[1])
    for k in range(1, nx):
        total = total + fx_recv[k - 1].astype(f32)
    dz_send[0] = total.astype(bf16)
    send(dz_send.at[0], dz_recv.at[0], 13, dz_sem.at[0], right)
    arrived(pre.at[core, 0 : ny - 1, 0 : near * per], c2_sem.at[ny - 1])
    for g in range(near):
        for k in range(1, ny):
            block = part_of(core, y_back(k), g)
            send(block, block, 10, c3_sem.at[1], partner)
    packed(pre, core, pre_full)
    part = back(pre_full[core], core)
    arrived(pre.at[other, :, 0 : near * per], c3_sem.at[1])
    packed(pre, other, pre_full)
    part = part + back(pre_full[other], other)
    dx_part[...] = part.reshape(dx_part.shape)
    for k in range(1, nx):
        for g in range(near):
            dx_send[k - 1, g] = dx_part[lax.rem(x + k, nx), groups[g]].astype(bf16)
        send(dx_send.at[k - 1], dx_recv.at[k - 1], 12, dx_sem.at[0], x_peer[k])
    arrived(dx_recv, dx_sem.at[0])
    for g in range(near):
        total = dx_part[x, groups[g]]
        for k in range(1, nx):
            total = total + dx_recv[k - 1, g].astype(f32)
        dz_part[g] = total
    dz_send[1] = dz_part[1].astype(bf16)
    send(dz_send.at[1], dz_recv.at[1], 13, dz_sem.at[1], left)
    arrived(dz_recv.at[0], dz_sem.at[0])
    dz_send[2] = (dz_part[2] + dz_recv[0].astype(f32)).astype(bf16)
    send(dz_send.at[2], dz_recv.at[2], 13, dz_sem.at[2], right)

    def outer(a, b):
        return lax.dot_general(
            a[...], b, (((0,), (0,)), ((), ())), preferred_element_type=f32
        ).astype(bf16)

    for i in range(2):
        gwi_v[:, i * half : (i + 1) * half] = outer(input_rows, pre_full[i])
    arrived(hid.at[other], hc_sem.at[0])
    for i in range(2):
        packed(hid, i, hid_full)
        gwo_v[:, i * half : (i + 1) * half] = outer(grad_rows, hid_full[i])
    arrived(dz_recv.at[1], dz_sem.at[1])
    arrived(dz_recv.at[2], dz_sem.at[2])
    gin_v[...] = (dz_part[0] + dz_recv[1].astype(f32) + dz_recv[2].astype(f32)).astype(bf16)
    sent = (
        rows.at[0 : 3 + nh * (nx - 1)], peer_s, b1_send, b2_send, b3_send.at[0 : nz - 1],
        hid.at[core, y, 0 : nz - 1], pre.at[core, y, 0 : nz - 1], hid.at[core, 0 : ny - 1],
        hid.at[core], pre.at[core, 0 : ny - 1], pre.at[core], fx_send, dx_send, dz_send, saved_send,
    )
    for group, ref in enumerate(sent):
        handle(ref, group, s_sem.at[0]).wait_send()


def put(*refs):
    sems = refs[6]
    copies = [pltpu.make_async_copy(refs[i], refs[3 + i], sems.at[i]) for i in range(3)]
    for copy in copies:
        copy.start()
    for copy in copies:
        copy.wait()


def on_device(inputs, grad_out, saved_pre, w_in, w_out):
    ny, nz, nx, nh = (GRID[k] for k in ("ny", "nz", "nx", "nh"))
    step, width = inputs.shape
    n, hidden = saved_pre.shape
    half = hidden // 2
    tokens = step * nx * nh
    deep = tokens // (ny * nz)
    vmem, dma = pltpu.VMEM, pltpu.SemaphoreType.DMA
    shapes = ((step, width), (width, hidden), (width, hidden))
    any_space = pl.BlockSpec(memory_space=pl.ANY)
    results = pl.pallas_call(
        functools.partial(kernel, ny, nz, nx, nh),
        out_shape=tuple(vmem(shape, bf16) for shape in shapes),
        in_specs=[any_space] * 5,
        out_specs=(pl.BlockSpec(memory_space=vmem),) * 3,
        scratch_shapes=[
            vmem((nx * nh, 2, step, width), bf16),
            vmem((2, n, half), bf16),
            vmem((n, half), bf16),
            vmem((2, width, half), bf16),
            vmem((2, width, half), bf16),
            vmem((tokens, width), f32),
            vmem((tokens, width), bf16),
            vmem((tokens, width), bf16),
            vmem((deep, half), f32),
            vmem((deep, half), f32),
            vmem((deep, half), bf16),
            vmem((deep, half), bf16),
            vmem((2, ny, nz, deep, half), bf16),
            vmem((2, ny, nz, deep, half), bf16),
            vmem((ny, nh, step, half), bf16),
            vmem((ny, nh, step, half), bf16),
            vmem((ny, nh, step, half), f32),
            vmem((ny - 1, nh, step, half), bf16),
            vmem((ny - 1, nh, step, half), bf16),
            vmem((nh, step, half), f32),
            vmem((nz, deep, half), bf16),
            vmem((nz, deep, half), f32),
            vmem((nz, deep, half), bf16),
            vmem((tokens, half), f32),
            vmem((2, tokens, half), bf16),
            vmem((2, tokens, half), bf16),
            vmem((nx, step, width), f32),
            vmem((nx - 1, step, width), bf16),
            vmem((nx - 1, step, width), bf16),
            vmem((nx, nh, step, width), f32),
            vmem((nx - 1, nh - 1, step, width), bf16),
            vmem((nx - 1, nh - 1, step, width), bf16),
            vmem((nh - 1, step, width), f32),
            vmem((3, step, width), bf16),
            vmem((3, step, width), bf16),
            dma((5,)),
            dma((15,)),
            dma((3,)),
            dma((2,)),
            dma((1,)),
            dma((1,)),
            dma((1,)),
            dma((1,)),
            dma((1,)),
            dma((ny + 1,)),
            dma((2,)),
            dma((1,)),
            dma((nz,)),
            dma((ny,)),
            dma((2,)),
            dma((2,)),
            dma((3,)),
        ],
        compiler_params=pltpu.CompilerParams(
            collective_id=0, has_side_effects=True
        ),
    )(inputs, grad_out, saved_pre, w_in, w_out.T)
    grad_in, grad_w_in, grad_w_out = pl.pallas_call(
        put,
        out_shape=tuple(jax.ShapeDtypeStruct(shape, bf16) for shape in shapes),
        in_specs=[pl.BlockSpec(memory_space=vmem)] * 3,
        out_specs=(any_space,) * 3,
        scratch_shapes=[dma((3,))],
    )(*[pltpu.with_memory_space_constraint(r, vmem) for r in results])
    return grad_in, grad_w_in, grad_w_out.T


def solution(mesh):
    return jax.shard_map(
        on_device,
        mesh=mesh,
        in_specs=(
            P("tensor", "dp"),
            P("tensor", "dp"),
            P("dp", "tensor"),
            P("dp", "tensor"),
            P("tensor", "dp"),
        ),
        out_specs=(P("tensor", "dp"), P("dp", "tensor"), P("tensor", "dp")),
        check_vma=False,
    )
```

```python
import functools

import jax
import jax.numpy as jnp
from jax import lax
from jax.experimental import pallas as pl
from jax.experimental.pallas import tpu as pltpu
from jax.sharding import PartitionSpec as P

GRID = dict(ny=4, nz=8, nx=4, nh=4)

root_half = 0.7071067811865476
inv_root_two_pi = 0.3989422804014327
bf16, f32 = jnp.bfloat16, jnp.float32


def gelu_parts(saved):
    value = saved.astype(f32)
    cdf = 0.5 * (1.0 + lax.erf(value * root_half))
    density = inv_root_two_pi * jnp.exp(-0.5 * value * value)
    return value * cdf, cdf + value * density


def kernel(
    ny, nz, nx, nh,
    x_hbm, g_hbm, s_hbm, wi_hbm, wo_hbm,
    gin_v, gwi_v, gwo_v,
    rows, own_s, peer_s, wi_v, wo_v, wide, grad_rows, input_rows,
    slope, quad, saved_send, saved_recv, hid, pre,
    b1_send, b1_recv, b1_own, b2_send, b2_recv, b2_sum, b3_send, b3_own, b3_recv,
    pack, hid_full, pre_full,
    fx_part, fx_send, fx_recv, dx_part, dx_send, dx_recv, dz_part, dz_send, dz_recv,
    local_sem, send_sem,
    az_sem, ax_sem, s_sem, sv_sem, hz_sem, hy_sem, hc_sem,
    b1_sem, b2_sem, b3_sem, c1_sem, c2_sem, c3_sem, dx_sem, dz_sem,
):
    dp, tp = lax.axis_index("dp"), lax.axis_index("tensor")
    core = lax.rem(dp, 2)
    chip = lax.div(dp, 2)
    z, y = lax.rem(chip, nz), lax.div(chip, nz)
    x, h = lax.div(tp, nh), lax.rem(tp, nh)
    other = 1 - core

    def at(y=y, z=z, core=core, x=x, h=h):
        return {"dp": (y * nz + z) * 2 + core, "tensor": x * nh + h}

    y_peer = [None] + [at(y=lax.rem(y + k, ny)) for k in range(1, ny)]
    z_peer = [None] + [at(z=lax.rem(z + k, nz)) for k in range(1, nz)]
    x_peer = [None] + [at(x=lax.rem(x + k, nx)) for k in range(1, nx)]
    right, left = at(h=lax.rem(h + 1, nh)), at(h=lax.rem(h + nh - 1, nh))
    partner = at(core=other)
    peers = y_peer[1:] + z_peer[1:] + x_peer[1:] + [right, left, partner]

    def far_to_near(n):
        return sorted(range(1, n), key=lambda k: -min(k, n - k))

    half = wi_v.shape[2]

    def load(src, dst, i):
        copy = pltpu.make_async_copy(src, dst, local_sem.at[i])
        copy.start()
        return copy

    load_g = load(g_hbm, rows.at[tp, 0], 0)
    load_x = load(x_hbm, rows.at[tp, 1], 1)
    for i in range(2):
        columns = pl.ds(i * half, half)
        for hbm, ref, sem in ((s_hbm, own_s, 2), (wo_hbm, wo_v, 3), (wi_hbm, wi_v, 4)):
            load(hbm.at[:, columns], ref.at[i], sem)

    def loaded(ref, sem):
        pltpu.make_async_copy(ref, ref, local_sem.at[sem]).wait()

    barrier = pltpu.get_barrier_semaphore()
    for peer in peers:
        pl.semaphore_signal(barrier, inc=1, device_id=peer, device_id_type=pl.DeviceIdType.MESH)
    pl.semaphore_wait(barrier, len(peers))

    def send(src, dst, group, recv_sem, peer):
        pltpu.make_async_remote_copy(
            src_ref=src, dst_ref=dst, send_sem=send_sem.at[group], recv_sem=recv_sem,
            device_id=peer, device_id_type=pl.DeviceIdType.MESH,
        ).start()

    def handle(ref, group, recv_sem):
        return pltpu.make_async_remote_copy(
            src_ref=ref, dst_ref=ref, send_sem=send_sem.at[group], recv_sem=recv_sem,
            device_id=partner, device_id_type=pl.DeviceIdType.MESH,
        )

    def arrived(ref, recv_sem):
        handle(ref, 0, recv_sem).wait_recv()

    slot = lambda x_, h_: x_ * nh + h_
    h_left, h_right, h_far = lax.rem(h + nh - 1, nh), lax.rem(h + 1, nh), lax.rem(h + 2, nh)

    def to_x(which, h_):
        block = rows.at[slot(x, h_)]
        for k in far_to_near(nx):
            send(block, block, 0, ax_sem.at[0 if which < nh - 1 else 1], x_peer[k])

    load_g.wait()
    load_x.wait()
    mine = rows.at[tp]
    send(mine, mine, 0, az_sem.at[0], right)
    send(mine, mine, 0, az_sem.at[1], left)

    loaded(own_s, 2)
    send(own_s.at[other], peer_s, 1, s_sem.at[0], partner)
    to_x(0, h)

    arrived(peer_s, s_sem.at[0])
    step, deep = rows.shape[2], b3_own.shape[1]
    per = step // deep
    shift = lax.rem(nz // 2 - 1 - per * h_far + nz, nz)
    middle = [nz // 2 - 1 + i for i in range(per)]
    outside = [i for i in range(nz) if i not in middle]

    def piece_of(z_):
        return lax.rem(z_ + nz - shift, nz)

    own, peer = own_s[core].astype(f32), peer_s[...].astype(f32)
    n = own.shape[0]
    first = core == 0
    quad[0:n, :] = jnp.where(first, own, peer)
    quad[n : 2 * n, :] = jnp.where(first, peer, own)
    saved_send[...] = quad[...].astype(bf16)
    send(saved_send, saved_recv, 14, sv_sem.at[0], at(z=lax.rem(z + shift, nz)))
    hid[core, y, z] = gelu_parts(quad[...])[0].astype(bf16)

    def to_z(block, group, sem):
        for k in far_to_near(nz):
            send(block, block, group, sem, z_peer[k])

    def from_z(buf, sem):
        arrived(buf.at[core, y, 0 : nz - 1], sem.at[0])

    from_left = rows.at[slot(x, h_left)]
    arrived(from_left, az_sem.at[0])
    send(from_left, from_left, 0, az_sem.at[2], right)
    to_x(1, h_left)
    arrived(rows.at[slot(x, h_right)], az_sem.at[1])
    to_x(2, h_right)
    near = nh - 1
    groups = (h, h_left, h_right, h_far)

    def product(lo, hi):
        count = (hi - lo) * nx
        for g in range(lo, hi):
            for x_ in range(nx):
                r = ((g - lo) * nx + x_) * step
                wide[r : r + step, :] = rows[slot(x_, groups[g]), 0].astype(f32)
        lhs = wide[0 : count * step, :].astype(bf16)

        def place(ref, which):
            out = jnp.dot(lhs, wo_v[which], preferred_element_type=f32).reshape(count, step, half)
            for g in range(lo, hi):
                for x_ in range(nx):
                    ref[x_, g] = out[(g - lo) * nx + x_].astype(ref.dtype)

        place(b1_send, other)
        for k in order:
            y_ = lax.rem(y + k, ny)
            send(b1_send.at[y_, lo:hi], b1_recv.at[y_, lo:hi], 2, b1_sem.at[ny if lo else k], partner)
        place(b1_own, core)

    def fold(lo, hi):
        if lo:
            arrived(b1_recv.at[:, lo:hi], b1_sem.at[ny])
        for k in order:
            y_ = lax.rem(y + k, ny)
            if lo == 0:
                arrived(b1_recv.at[y_, lo:hi], b1_sem.at[k])
            total = b1_own[y_, lo:hi] + b1_recv[y_, lo:hi].astype(f32)
            if k:
                b2_send[k - 1, lo:hi] = total.astype(bf16)
                send(b2_send.at[k - 1, lo:hi], b2_recv.at[k - 1, lo:hi], 3, b2_sem.at[1 if lo else 0], y_peer[k])
            else:
                b2_sum[lo:hi] = total

    order = far_to_near(ny) + [0]
    arrived(rows.at[0 : near * (nx - 1)], ax_sem.at[0])
    loaded(wo_v, 3)
    product(0, near)
    fold(0, near)
    arrived(rows.at[slot(x, h_far)], az_sem.at[2])
    to_x(near, h_far)
    to_z(hid.at[core, y, z], 5, hz_sem.at[0])
    arrived(rows.at[0 : nx - 1], ax_sem.at[1])
    product(near, nh)
    fold(near, nh)
    for lo, hi, owners in ((0, near, outside), (near, nh, middle)):
        arrived(b2_recv.at[:, lo:hi], b2_sem.at[1 if lo else 0])
        for g in range(lo, hi):
            total = b2_sum[g]
            for k in range(1, ny):
                total = total + b2_recv[k - 1, g].astype(f32)
            b2_sum[g] = total
            for i in range(per):
                piece = b2_sum[g, i * deep : (i + 1) * deep, :]
                b3_own[groups[g] * per + i] = piece
                b3_send[groups[g] * per + i] = piece.astype(bf16)
        for owner in owners:

            @pl.when(z != owner)
            def _():
                send(b3_send.at[piece_of(owner)], b3_recv.at[z], 4, b3_sem.at[0], at(z=owner))
    mine = piece_of(z)
    arrived(saved_recv, sv_sem.at[0])
    slope[...] = gelu_parts(saved_recv[...])[1]
    from_z(hid, hz_sem)
    for k in range(1, ny):
        send(hid.at[core, y], hid.at[core, y], 7, hy_sem.at[0], y_peer[k])
    total = b3_own[mine]
    arrived(b3_recv.at[0 : nz - 1], b3_sem.at[0])
    for k in range(1, nz):
        total = total + b3_recv[lax.rem(z + k, nz)].astype(f32)
    pre[core, y, mine] = (total * slope[...]).astype(bf16)
    def gathered(which, out):
        for t in range(rows.shape[0]):
            wide[t * step : (t + 1) * step, :] = rows[t, which].astype(f32)
        out[...] = wide[...].astype(bf16)

    to_z(pre.at[core, y, mine], 6, c1_sem.at[z])
    gathered(0, grad_rows)
    gathered(1, input_rows)

    def from_owners(owners):
        for owner in owners:

            @pl.when(z != owner)
            def _():
                arrived(pre.at[core, y, piece_of(owner)], c1_sem.at[owner])

    from_owners(middle)

    def part_of(half_, y_, g):
        return pre.at[half_, y_, pl.ds(groups[g] * per, per)]

    def y_back(k):
        return lax.rem(y + ny - k, ny)

    def to_y(g):
        block = part_of(core, y, g)
        for k in far_to_near(ny):
            send(block, block, 9, c2_sem.at[k - 1 if g == near else ny - 1], y_peer[k])
        send(block, block, 10, c3_sem.at[0 if g == near else 1], partner)

    to_y(near)
    arrived(hid.at[core, 0 : ny - 1], hy_sem.at[0])
    send(hid.at[core], hid.at[core], 8, hc_sem.at[0], partner)

    def packed(buf, which, out):
        for i in range(ny):
            for j in range(nz):
                r = (i * nz + j) * deep
                pack[r : r + deep, :] = buf[which, i, j].astype(f32)
        out[which] = pack[...].astype(bf16)

    def back(lhs, which):
        return lax.dot_general(lhs, wi_v[which], (((1,), (1,)), ((), ())), preferred_element_type=f32)

    def far_back(which):
        for i in range(ny):
            for j in range(per):
                r = i * step + j * deep
                pack[r : r + deep, :] = pre[which, i, h_far * per + j].astype(f32)
        return back(pack[0 : ny * step, :].astype(bf16), which)

    for k in range(1, ny):
        block = part_of(core, y_back(k), near)
        arrived(block, c2_sem.at[k - 1])
        send(block, block, 10, c3_sem.at[0], partner)
    from_owners(outside)
    for g in range(near):
        to_y(g)
    loaded(wi_v, 4)
    part = far_back(core)
    arrived(pre.at[other, :, 0:per], c3_sem.at[0])
    part = part + far_back(other)

    fx_part[...] = part.reshape(fx_part.shape)
    for k in far_to_near(nx):
        fx_send[k - 1] = fx_part[lax.rem(x + k, nx)].astype(bf16)
        send(fx_send.at[k - 1], fx_recv.at[k - 1], 11, dx_sem.at[1], x_peer[k])
    total = fx_part[x]
    arrived(fx_recv, dx_sem.at[1])
    for k in range(1, nx):
        total = total + fx_recv[k - 1].astype(f32)
    dz_send[0] = total.astype(bf16)
    send(dz_send.at[0], dz_recv.at[0], 13, dz_sem.at[0], right)
    arrived(pre.at[core, 0 : ny - 1, 0 : near * per], c2_sem.at[ny - 1])
    for g in range(near):
        for k in range(1, ny):
            block = part_of(core, y_back(k), g)
            send(block, block, 10, c3_sem.at[1], partner)
    packed(pre, core, pre_full)
    part = back(pre_full[core], core)
    arrived(pre.at[other, :, 0 : near * per], c3_sem.at[1])
    packed(pre, other, pre_full)
    part = part + back(pre_full[other], other)
    dx_part[...] = part.reshape(dx_part.shape)
    for k in range(1, nx):
        for g in range(near):
            dx_send[k - 1, g] = dx_part[lax.rem(x + k, nx), groups[g]].astype(bf16)
        send(dx_send.at[k - 1], dx_recv.at[k - 1], 12, dx_sem.at[0], x_peer[k])
    arrived(dx_recv, dx_sem.at[0])
    for g in range(near):
        total = dx_part[x, groups[g]]
        for k in range(1, nx):
            total = total + dx_recv[k - 1, g].astype(f32)
        dz_part[g] = total
    dz_send[1] = dz_part[1].astype(bf16)
    send(dz_send.at[1], dz_recv.at[1], 13, dz_sem.at[1], left)
    arrived(dz_recv.at[0], dz_sem.at[0])
    dz_send[2] = (dz_part[2] + dz_recv[0].astype(f32)).astype(bf16)
    send(dz_send.at[2], dz_recv.at[2], 13, dz_sem.at[2], right)

    def outer(a, b):
        return lax.dot_general(
            a[...], b, (((0,), (0,)), ((), ())), preferred_element_type=f32
        ).astype(bf16)

    for i in range(2):
        gwi_v[:, i * half : (i + 1) * half] = outer(input_rows, pre_full[i])
    arrived(hid.at[other], hc_sem.at[0])
    for i in range(2):
        packed(hid, i, hid_full)
        gwo_v[:, i * half : (i + 1) * half] = outer(grad_rows, hid_full[i])
    arrived(dz_recv.at[1], dz_sem.at[1])
    arrived(dz_recv.at[2], dz_sem.at[2])
    gin_v[...] = (dz_part[0] + dz_recv[1].astype(f32) + dz_recv[2].astype(f32)).astype(bf16)
    sent = (
        rows.at[0 : 3 + nh * (nx - 1)], peer_s, b1_send, b2_send, b3_send.at[0 : nz - 1],
        hid.at[core, y, 0 : nz - 1], pre.at[core, y, 0 : nz - 1], hid.at[core, 0 : ny - 1],
        hid.at[core], pre.at[core, 0 : ny - 1], pre.at[core], fx_send, dx_send, dz_send, saved_send,
    )
    for group, ref in enumerate(sent):
        handle(ref, group, s_sem.at[0]).wait_send()


def put(*refs):
    sems = refs[6]
    copies = [pltpu.make_async_copy(refs[i], refs[3 + i], sems.at[i]) for i in range(3)]
    for copy in copies:
        copy.start()
    for copy in copies:
        copy.wait()


def on_device(inputs, grad_out, saved_pre, w_in, w_out):
    ny, nz, nx, nh = (GRID[k] for k in ("ny", "nz", "nx", "nh"))
    step, width = inputs.shape
    n, hidden = saved_pre.shape
    half = hidden // 2
    tokens = step * nx * nh
    deep = tokens // (ny * nz)
    vmem, dma = pltpu.VMEM, pltpu.SemaphoreType.DMA
    shapes = ((step, width), (width, hidden), (width, hidden))
    any_space = pl.BlockSpec(memory_space=pl.ANY)
    results = pl.pallas_call(
        functools.partial(kernel, ny, nz, nx, nh),
        out_shape=tuple(vmem(shape, bf16) for shape in shapes),
        in_specs=[any_space] * 5,
        out_specs=(pl.BlockSpec(memory_space=vmem),) * 3,
        scratch_shapes=[
            vmem((nx * nh, 2, step, width), bf16),
            vmem((2, n, half), bf16),
            vmem((n, half), bf16),
            vmem((2, width, half), bf16),
            vmem((2, width, half), bf16),
            vmem((tokens, width), f32),
            vmem((tokens, width), bf16),
            vmem((tokens, width), bf16),
            vmem((deep, half), f32),
            vmem((deep, half), f32),
            vmem((deep, half), bf16),
            vmem((deep, half), bf16),
            vmem((2, ny, nz, deep, half), bf16),
            vmem((2, ny, nz, deep, half), bf16),
            vmem((ny, nh, step, half), bf16),
            vmem((ny, nh, step, half), bf16),
            vmem((ny, nh, step, half), f32),
            vmem((ny - 1, nh, step, half), bf16),
            vmem((ny - 1, nh, step, half), bf16),
            vmem((nh, step, half), f32),
            vmem((nz, deep, half), bf16),
            vmem((nz, deep, half), f32),
            vmem((nz, deep, half), bf16),
            vmem((tokens, half), f32),
            vmem((2, tokens, half), bf16),
            vmem((2, tokens, half), bf16),
            vmem((nx, step, width), f32),
            vmem((nx - 1, step, width), bf16),
            vmem((nx - 1, step, width), bf16),
            vmem((nx, nh, step, width), f32),
            vmem((nx - 1, nh - 1, step, width), bf16),
            vmem((nx - 1, nh - 1, step, width), bf16),
            vmem((nh - 1, step, width), f32),
            vmem((3, step, width), bf16),
            vmem((3, step, width), bf16),
            dma((5,)),
            dma((15,)),
            dma((3,)),
            dma((2,)),
            dma((1,)),
            dma((1,)),
            dma((1,)),
            dma((1,)),
            dma((1,)),
            dma((ny + 1,)),
            dma((2,)),
            dma((1,)),
            dma((nz,)),
            dma((ny,)),
            dma((2,)),
            dma((2,)),
            dma((3,)),
        ],
        compiler_params=pltpu.CompilerParams(
            collective_id=0, has_side_effects=True
        ),
    )(inputs, grad_out, saved_pre, w_in, w_out.T)
    grad_in, grad_w_in, grad_w_out = pl.pallas_call(
        put,
        out_shape=tuple(jax.ShapeDtypeStruct(shape, bf16) for shape in shapes),
        in_specs=[pl.BlockSpec(memory_space=vmem)] * 3,
        out_specs=(any_space,) * 3,
        scratch_shapes=[dma((3,))],
    )(*[pltpu.with_memory_space_constraint(r, vmem) for r in results])
    return grad_in, grad_w_in, grad_w_out.T


def solution(mesh):
    return jax.shard_map(
        on_device,
        mesh=mesh,
        in_specs=(
            P("tensor", "dp"),
            P("tensor", "dp"),
            P("dp", "tensor"),
            P("dp", "tensor"),
            P("tensor", "dp"),
        ),
        out_specs=(P("tensor", "dp"), P("dp", "tensor"), P("tensor", "dp")),
        check_vma=False,
    )
```

```python
import functools

import jax
import jax.numpy as jnp
from jax import lax
from jax.experimental import pallas as pl
from jax.experimental.pallas import tpu as pltpu
from jax.sharding import PartitionSpec as P

GRID = dict(ny=4, nz=8, nx=4, nh=4)

root_half = 0.7071067811865476
inv_root_two_pi = 0.3989422804014327
bf16, f32 = jnp.bfloat16, jnp.float32


def gelu_parts(saved):
    value = saved.astype(f32)
    cdf = 0.5 * (1.0 + lax.erf(value * root_half))
    density = inv_root_two_pi * jnp.exp(-0.5 * value * value)
    return value * cdf, cdf + value * density


def kernel(
    ny, nz, nx, nh,
    x_hbm, g_hbm, s_hbm, wi_hbm, wo_hbm,
    gin_v, gwi_v, gwo_v,
    rows, own_s, peer_s, wi_v, wo_v, wide, grad_rows, input_rows,
    slope, quad, saved_send, saved_recv, hid, pre,
    b1_send, b1_recv, b1_own, b2_send, b2_recv, b2_sum, b3_send, b3_own, b3_recv,
    pack, hid_full, pre_full,
    fx_part, fx_send, fx_recv, dx_part, dx_send, dx_recv, dz_part, dz_send, dz_recv,
    local_sem, send_sem,
    az_sem, ax_sem, s_sem, sv_sem, hz_sem, hy_sem, hc_sem,
    b1_sem, b2_sem, b3_sem, c1_sem, c2_sem, c3_sem, dx_sem, dz_sem,
):
    dp, tp = lax.axis_index("dp"), lax.axis_index("tensor")
    core = lax.rem(dp, 2)
    chip = lax.div(dp, 2)
    z, y = lax.rem(chip, nz), lax.div(chip, nz)
    x, h = lax.div(tp, nh), lax.rem(tp, nh)
    other = 1 - core

    def at(y=y, z=z, core=core, x=x, h=h):
        return {"dp": (y * nz + z) * 2 + core, "tensor": x * nh + h}

    y_peer = [None] + [at(y=lax.rem(y + k, ny)) for k in range(1, ny)]
    z_peer = [None] + [at(z=lax.rem(z + k, nz)) for k in range(1, nz)]
    x_peer = [None] + [at(x=lax.rem(x + k, nx)) for k in range(1, nx)]
    right, left = at(h=lax.rem(h + 1, nh)), at(h=lax.rem(h + nh - 1, nh))
    partner, opposite = at(core=other), at(h=lax.rem(h + 2, nh))
    peers = y_peer[1:] + z_peer[1:] + x_peer[1:] + [right, left, partner]

    def far_to_near(n):
        return sorted(range(1, n), key=lambda k: -min(k, n - k))

    half = wi_v.shape[2]

    def load(src, dst, i):
        copy = pltpu.make_async_copy(src, dst, local_sem.at[i])
        copy.start()
        return copy

    load_g = load(g_hbm, rows.at[tp, 0], 0)
    load_x = load(x_hbm, rows.at[tp, 1], 1)
    for i in range(2):
        columns = pl.ds(i * half, half)
        for hbm, ref, sem in ((s_hbm, own_s, 2), (wo_hbm, wo_v, 3), (wi_hbm, wi_v, 4)):
            load(hbm.at[:, columns], ref.at[i], sem)

    def loaded(ref, sem):
        pltpu.make_async_copy(ref, ref, local_sem.at[sem]).wait()

    barrier = pltpu.get_barrier_semaphore()
    for peer in peers:
        pl.semaphore_signal(barrier, inc=1, device_id=peer, device_id_type=pl.DeviceIdType.MESH)
    pl.semaphore_wait(barrier, len(peers))

    def send(src, dst, group, recv_sem, peer):
        pltpu.make_async_remote_copy(
            src_ref=src, dst_ref=dst, send_sem=send_sem.at[group], recv_sem=recv_sem,
            device_id=peer, device_id_type=pl.DeviceIdType.MESH,
        ).start()

    def handle(ref, group, recv_sem):
        return pltpu.make_async_remote_copy(
            src_ref=ref, dst_ref=ref, send_sem=send_sem.at[group], recv_sem=recv_sem,
            device_id=partner, device_id_type=pl.DeviceIdType.MESH,
        )

    def arrived(ref, recv_sem):
        handle(ref, 0, recv_sem).wait_recv()

    slot = lambda x_, h_: x_ * nh + h_
    h_left, h_right, h_far = lax.rem(h + nh - 1, nh), lax.rem(h + 1, nh), lax.rem(h + 2, nh)

    def to_x(which, h_):
        block = rows.at[slot(x, h_)]
        for k in far_to_near(nx):
            send(block, block, 0, ax_sem.at[0 if which < nh - 1 else 1], x_peer[k])

    load_g.wait()
    load_x.wait()
    mine = rows.at[tp]
    send(mine, mine, 0, az_sem.at[0], right)
    send(mine, mine, 0, az_sem.at[1], left)

    loaded(own_s, 2)
    send(own_s.at[other], peer_s, 1, s_sem.at[0], partner)
    to_x(0, h)

    arrived(peer_s, s_sem.at[0])
    step, deep = rows.shape[2], b3_own.shape[1]
    per = step // deep
    shift = lax.rem(nz // 2 - 1 - per * h_far + nz, nz)
    middle = [nz // 2 - 1 + i for i in range(per)]
    outside = [i for i in range(nz) if i not in middle]

    def piece_of(z_):
        return lax.rem(z_ + nz - shift, nz)

    own, peer = own_s[core].astype(f32), peer_s[...].astype(f32)
    n = own.shape[0]
    first = core == 0
    quad[0:n, :] = jnp.where(first, own, peer)
    quad[n : 2 * n, :] = jnp.where(first, peer, own)
    saved_send[...] = quad[...].astype(bf16)
    send(saved_send, saved_recv, 14, sv_sem.at[0], at(z=lax.rem(z + shift, nz)))
    hid[core, y, z] = gelu_parts(quad[...])[0].astype(bf16)

    def to_z(block, group, sem):
        for k in far_to_near(nz):
            send(block, block, group, sem, z_peer[k])

    def from_z(buf, sem):
        arrived(buf.at[core, y, 0 : nz - 1], sem.at[0])

    from_left = rows.at[slot(x, h_left)]
    arrived(from_left, az_sem.at[0])
    send(from_left, from_left, 0, az_sem.at[2], right)
    to_x(1, h_left)
    arrived(rows.at[slot(x, h_right)], az_sem.at[1])
    to_x(2, h_right)
    near = nh - 1
    groups = (h, h_left, h_right, h_far)

    def product(lo, hi):
        count = (hi - lo) * nx
        for g in range(lo, hi):
            for x_ in range(nx):
                r = ((g - lo) * nx + x_) * step
                wide[r : r + step, :] = rows[slot(x_, groups[g]), 0].astype(f32)
        lhs = wide[0 : count * step, :].astype(bf16)

        def place(ref, which):
            out = jnp.dot(lhs, wo_v[which], preferred_element_type=f32).reshape(count, step, half)
            for g in range(lo, hi):
                for x_ in range(nx):
                    ref[x_, g] = out[(g - lo) * nx + x_].astype(ref.dtype)

        place(b1_send, other)
        for k in order:
            y_ = lax.rem(y + k, ny)
            send(b1_send.at[y_, lo:hi], b1_recv.at[y_, lo:hi], 2, b1_sem.at[ny if lo else k], partner)
        place(b1_own, core)

    def fold(lo, hi):
        if lo:
            arrived(b1_recv.at[:, lo:hi], b1_sem.at[ny])
        for k in order:
            y_ = lax.rem(y + k, ny)
            if lo == 0:
                arrived(b1_recv.at[y_, lo:hi], b1_sem.at[k])
            total = b1_own[y_, lo:hi] + b1_recv[y_, lo:hi].astype(f32)
            if k:
                b2_send[k - 1, lo:hi] = total.astype(bf16)
                send(b2_send.at[k - 1, lo:hi], b2_recv.at[k - 1, lo:hi], 3, b2_sem.at[1 if lo else 0], y_peer[k])
            else:
                b2_sum[lo:hi] = total

    order = far_to_near(ny) + [0]
    arrived(rows.at[0 : near * (nx - 1)], ax_sem.at[0])
    loaded(wo_v, 3)
    product(0, near)
    fold(0, near)
    arrived(rows.at[slot(x, h_far)], az_sem.at[2])
    to_x(near, h_far)
    to_z(hid.at[core, y, z], 5, hz_sem.at[0])
    arrived(rows.at[0 : nx - 1], ax_sem.at[1])
    product(near, nh)
    fold(near, nh)
    for lo, hi, owners in ((0, near, outside), (near, nh, middle)):
        arrived(b2_recv.at[:, lo:hi], b2_sem.at[1 if lo else 0])
        for g in range(lo, hi):
            total = b2_sum[g]
            for k in range(1, ny):
                total = total + b2_recv[k - 1, g].astype(f32)
            b2_sum[g] = total
            for i in range(per):
                piece = b2_sum[g, i * deep : (i + 1) * deep, :]
                b3_own[groups[g] * per + i] = piece
                b3_send[groups[g] * per + i] = piece.astype(bf16)
        for owner in owners:

            @pl.when(z != owner)
            def _():
                send(b3_send.at[piece_of(owner)], b3_recv.at[z], 4, b3_sem.at[0], at(z=owner))
    mine = piece_of(z)
    arrived(saved_recv, sv_sem.at[0])
    slope[...] = gelu_parts(saved_recv[...])[1]
    from_z(hid, hz_sem)
    for k in range(1, ny):
        send(hid.at[core, y], hid.at[core, y], 7, hy_sem.at[0], y_peer[k])
    total = b3_own[mine]
    arrived(b3_recv.at[0 : nz - 1], b3_sem.at[0])
    for k in range(1, nz):
        total = total + b3_recv[lax.rem(z + k, nz)].astype(f32)
    pre[core, y, mine] = (total * slope[...]).astype(bf16)
    def gathered(which, out):
        for t in range(rows.shape[0]):
            wide[t * step : (t + 1) * step, :] = rows[t, which].astype(f32)
        out[...] = wide[...].astype(bf16)

    to_z(pre.at[core, y, mine], 6, c1_sem.at[z])
    gathered(0, grad_rows)
    gathered(1, input_rows)

    def from_owners(owners):
        for owner in owners:

            @pl.when(z != owner)
            def _():
                arrived(pre.at[core, y, piece_of(owner)], c1_sem.at[owner])

    from_owners(middle)

    def part_of(half_, y_, g):
        return pre.at[half_, y_, pl.ds(groups[g] * per, per)]

    def y_back(k):
        return lax.rem(y + ny - k, ny)

    def to_y(g):
        block = part_of(core, y, g)
        for k in far_to_near(ny):
            send(block, block, 9, c2_sem.at[k - 1 if g == near else ny - 1], y_peer[k])
        send(block, block, 10, c3_sem.at[0 if g == near else 1], partner)

    to_y(near)
    arrived(hid.at[core, 0 : ny - 1], hy_sem.at[0])
    send(hid.at[core], hid.at[core], 8, hc_sem.at[0], partner)

    def packed(buf, which, out):
        for i in range(ny):
            for j in range(nz):
                r = (i * nz + j) * deep
                pack[r : r + deep, :] = buf[which, i, j].astype(f32)
        out[which] = pack[...].astype(bf16)

    def back(lhs, which):
        return lax.dot_general(lhs, wi_v[which], (((1,), (1,)), ((), ())), preferred_element_type=f32)

    def far_back(which):
        for i in range(ny):
            for j in range(per):
                r = i * step + j * deep
                pack[r : r + deep, :] = pre[which, i, h_far * per + j].astype(f32)
        return back(pack[0 : ny * step, :].astype(bf16), which)

    for k in range(1, ny):
        block = part_of(core, y_back(k), near)
        arrived(block, c2_sem.at[k - 1])
        send(block, block, 10, c3_sem.at[0], partner)
    from_owners(outside)
    for g in range(near):
        to_y(g)
    loaded(wi_v, 4)
    part = far_back(core)
    arrived(pre.at[other, :, 0:per], c3_sem.at[0])
    part = part + far_back(other)

    fx_part[...] = part.reshape(fx_part.shape)
    for k in far_to_near(nx):
        fx_send[k - 1] = fx_part[lax.rem(x + k, nx)].astype(bf16)
        send(fx_send.at[k - 1], fx_recv.at[k - 1], 11, dx_sem.at[1], x_peer[k])
    total = fx_part[x]
    arrived(fx_recv, dx_sem.at[1])
    for k in range(1, nx):
        total = total + fx_recv[k - 1].astype(f32)
    dz_send[0] = total.astype(bf16)
    send(dz_send.at[0], dz_recv.at[0], 13, dz_sem.at[0], opposite)
    arrived(pre.at[core, 0 : ny - 1, 0 : near * per], c2_sem.at[ny - 1])
    for g in range(near):
        for k in range(1, ny):
            block = part_of(core, y_back(k), g)
            send(block, block, 10, c3_sem.at[1], partner)
    packed(pre, core, pre_full)
    part = back(pre_full[core], core)
    arrived(pre.at[other, :, 0 : near * per], c3_sem.at[1])
    packed(pre, other, pre_full)
    part = part + back(pre_full[other], other)
    dx_part[...] = part.reshape(dx_part.shape)
    for k in range(1, nx):
        for g in range(near):
            dx_send[k - 1, g] = dx_part[lax.rem(x + k, nx), groups[g]].astype(bf16)
        send(dx_send.at[k - 1], dx_recv.at[k - 1], 12, dx_sem.at[0], x_peer[k])
    arrived(dx_recv, dx_sem.at[0])
    for g in range(near):
        total = dx_part[x, groups[g]]
        for k in range(1, nx):
            total = total + dx_recv[k - 1, g].astype(f32)
        dz_part[g] = total
    dz_send[1] = dz_part[1].astype(bf16)
    send(dz_send.at[1], dz_recv.at[1], 13, dz_sem.at[1], left)
    dz_send[2] = dz_part[2].astype(bf16)
    send(dz_send.at[2], dz_recv.at[2], 13, dz_sem.at[2], right)

    def outer(a, b):
        return lax.dot_general(
            a[...], b, (((0,), (0,)), ((), ())), preferred_element_type=f32
        ).astype(bf16)

    for i in range(2):
        gwi_v[:, i * half : (i + 1) * half] = outer(input_rows, pre_full[i])
    arrived(hid.at[other], hc_sem.at[0])
    for i in range(2):
        packed(hid, i, hid_full)
        gwo_v[:, i * half : (i + 1) * half] = outer(grad_rows, hid_full[i])
    arrived(dz_recv.at[1], dz_sem.at[1])
    arrived(dz_recv.at[2], dz_sem.at[2])
    arrived(dz_recv.at[0], dz_sem.at[0])
    total = dz_part[0]
    for i in range(3):
        total = total + dz_recv[i].astype(f32)
    gin_v[...] = total.astype(bf16)
    sent = (
        rows.at[0 : 3 + nh * (nx - 1)], peer_s, b1_send, b2_send, b3_send.at[0 : nz - 1],
        hid.at[core, y, 0 : nz - 1], pre.at[core, y, 0 : nz - 1], hid.at[core, 0 : ny - 1],
        hid.at[core], pre.at[core, 0 : ny - 1], pre.at[core], fx_send, dx_send, dz_send, saved_send,
    )
    for group, ref in enumerate(sent):
        handle(ref, group, s_sem.at[0]).wait_send()


def put(*refs):
    sems = refs[6]
    copies = [pltpu.make_async_copy(refs[i], refs[3 + i], sems.at[i]) for i in range(3)]
    for copy in copies:
        copy.start()
    for copy in copies:
        copy.wait()


def on_device(inputs, grad_out, saved_pre, w_in, w_out):
    ny, nz, nx, nh = (GRID[k] for k in ("ny", "nz", "nx", "nh"))
    step, width = inputs.shape
    n, hidden = saved_pre.shape
    half = hidden // 2
    tokens = step * nx * nh
    deep = tokens // (ny * nz)
    vmem, dma = pltpu.VMEM, pltpu.SemaphoreType.DMA
    shapes = ((step, width), (width, hidden), (width, hidden))
    any_space = pl.BlockSpec(memory_space=pl.ANY)
    results = pl.pallas_call(
        functools.partial(kernel, ny, nz, nx, nh),
        out_shape=tuple(vmem(shape, bf16) for shape in shapes),
        in_specs=[any_space] * 5,
        out_specs=(pl.BlockSpec(memory_space=vmem),) * 3,
        scratch_shapes=[
            vmem((nx * nh, 2, step, width), bf16),
            vmem((2, n, half), bf16),
            vmem((n, half), bf16),
            vmem((2, width, half), bf16),
            vmem((2, width, half), bf16),
            vmem((tokens, width), f32),
            vmem((tokens, width), bf16),
            vmem((tokens, width), bf16),
            vmem((deep, half), f32),
            vmem((deep, half), f32),
            vmem((deep, half), bf16),
            vmem((deep, half), bf16),
            vmem((2, ny, nz, deep, half), bf16),
            vmem((2, ny, nz, deep, half), bf16),
            vmem((ny, nh, step, half), bf16),
            vmem((ny, nh, step, half), bf16),
            vmem((ny, nh, step, half), f32),
            vmem((ny - 1, nh, step, half), bf16),
            vmem((ny - 1, nh, step, half), bf16),
            vmem((nh, step, half), f32),
            vmem((nz, deep, half), bf16),
            vmem((nz, deep, half), f32),
            vmem((nz, deep, half), bf16),
            vmem((tokens, half), f32),
            vmem((2, tokens, half), bf16),
            vmem((2, tokens, half), bf16),
            vmem((nx, step, width), f32),
            vmem((nx - 1, step, width), bf16),
            vmem((nx - 1, step, width), bf16),
            vmem((nx, nh, step, width), f32),
            vmem((nx - 1, nh - 1, step, width), bf16),
            vmem((nx - 1, nh - 1, step, width), bf16),
            vmem((nh - 1, step, width), f32),
            vmem((3, step, width), bf16),
            vmem((3, step, width), bf16),
            dma((5,)),
            dma((15,)),
            dma((3,)),
            dma((2,)),
            dma((1,)),
            dma((1,)),
            dma((1,)),
            dma((1,)),
            dma((1,)),
            dma((ny + 1,)),
            dma((2,)),
            dma((1,)),
            dma((nz,)),
            dma((ny,)),
            dma((2,)),
            dma((2,)),
            dma((3,)),
        ],
        compiler_params=pltpu.CompilerParams(
            collective_id=0, has_side_effects=True
        ),
    )(inputs, grad_out, saved_pre, w_in, w_out.T)
    grad_in, grad_w_in, grad_w_out = pl.pallas_call(
        put,
        out_shape=tuple(jax.ShapeDtypeStruct(shape, bf16) for shape in shapes),
        in_specs=[pl.BlockSpec(memory_space=vmem)] * 3,
        out_specs=(any_space,) * 3,
        scratch_shapes=[dma((3,))],
    )(*[pltpu.with_memory_space_constraint(r, vmem) for r in results])
    return grad_in, grad_w_in, grad_w_out.T


def solution(mesh):
    return jax.shard_map(
        on_device,
        mesh=mesh,
        in_specs=(
            P("tensor", "dp"),
            P("tensor", "dp"),
            P("dp", "tensor"),
            P("dp", "tensor"),
            P("tensor", "dp"),
        ),
        out_specs=(P("tensor", "dp"), P("dp", "tensor"), P("tensor", "dp")),
        check_vma=False,
    )
```
